256 devices in a mesh: bx: 8 (over z), by: 8 (over y, core), bz: 4 (over x).
Axes of the slice: x: 4, y: 4, z: 8, core: 2. Of those that a mesh axis runs over, the one named last changes fastest.
Arguments:
- positions: float32 [3, 1048576], P(None, ('bx', 'by', 'bz')), may hold values from -15 to 55, as said below
- velocities: float32 [3, 1048576], P(None, ('bx', 'by', 'bz')), may hold values from -6 to 6
- species: int32 [1048576], P(('bx', 'by', 'bz')), may hold values 0 or 1
- corner_slot: int32 [2, 8, 1048576], P(None, None, ('bx', 'by', 'bz')), may hold values from 0 to 255, as said below
- corner_weight: float32 [8, 1048576], P(None, ('bx', 'by', 'bz')), may hold values from 0 to 1, as said below
- slot_cell: int32 [3, 16384, 256], P(None, ('bx', 'by', 'bz')), may hold values from 0 to 63, as said below
- bond_pairs: int32 [2, 983040], P(None, ('bx', 'by', 'bz')), may hold values from 0 to 4095, as said below
Outputs:
- new_positions: float32 [3, 1048576], P(None, ('bx', 'by', 'bz'))
- new_velocities: float32 [3, 1048576], P(None, ('bx', 'by', 'bz'))
- smoothed: float32 [2, 128, 512, 256], P(None, 'bx', 'by', 'bz')
The draws below stay inside these ranges and needn't reach their ends.
Inputs may be any that keep to these rules, and one draw needn't show every extreme that they name: `corner_slot`: row 0 is below 64 and row 1 below 256. For every owner and destination brick the named slots are those below a count of at least 32; the count is 256 for some destination of every owner, and for some brick of every z plane from all owners of that plane. `corner_weight`: for each bead the eight weights are the trilinear weights of a point inside a cell, corner c taking the upper side along x, y, z by bits 4, 2, 1 of c; they sum to one. `slot_cell`: row 0 is below 16, row 1 below 64, row 2 below 64. `bond_pairs`: bonds join beads of one device into chains of 16 beads; each bead lies in at most two bonds. `positions`: bonded beads stand at distance 1.
All inputs are finite; a program needn't handle non-finite values. No bound on the sum of `species` on one device may be relied on, other than what follows from the above.
Results may differ from the reference program's by a relative error of at most 0.0003.
Values sent between devices are 32-bit elements; how exact they have to be, the bound alone decides.
A program may use at most 128 MiB of HBM per device.

```python
import math
import jax
import jax.numpy as jnp

CX = 16
CY = 64
CZ = 64
BEADS_DEV = 4096
MOL = 16
REACH = 3
SWEEPS = 4
SLOTS = 256
PLANE = 64
NX = 128
NY = 512
NZ = 256
BEADS = 1048576
BONDS_DEV = 3840
BONDS = 983040
N_BY = 8
N_BZ = 4
DEVICES = 256


def chain_layout(key, device):
    return jax.random.permutation(jax.random.fold_in(jax.random.fold_in(key, 4242), device), BEADS_DEV).astype(jnp.int32)


def draw_bond_pairs(key, part):

    def one_device(device):
        order = chain_layout(key, device).reshape(BEADS_DEV // MOL, MOL)
        return jnp.stack([order[:, :-1].reshape(-1), order[:, 1:].reshape(-1)])
    blocks = jax.vmap(one_device)(jnp.arange(DEVICES, dtype=jnp.int32))
    return jnp.transpose(blocks, (1, 0, 2)).reshape(2, -1).astype(jnp.int32)


def draw_positions(key, part):

    def one_device(device):
        branch_key = jax.random.fold_in(jax.random.fold_in(key, 5151), device)
        key_steps, key_starts = jax.random.split(branch_key, 2)
        chains = BEADS_DEV // MOL
        steps = jax.random.normal(key_steps, (chains, MOL, 3), jnp.float32)
        steps = steps / jnp.sqrt(jnp.sum(steps * steps, axis=-1, keepdims=True) + 1e-12)
        first_mask = (jnp.arange(MOL) > 0).astype(jnp.float32)[None, :, None]
        steps = steps * first_mask
        starts = jax.random.uniform(key_starts, (chains, 1, 3), jnp.float32, 0.0, 40.0)
        coords = starts + jnp.cumsum(steps, axis=1)
        order = chain_layout(key, device)
        return jnp.zeros((3, BEADS_DEV), jnp.float32).at[:, order].set(coords.reshape(-1, 3).T)
    blocks = jax.vmap(one_device)(jnp.arange(DEVICES, dtype=jnp.int32))
    return jnp.transpose(blocks, (1, 0, 2)).reshape(3, -1)


def draw_corner_weight(key, part):
    fraction = jax.random.uniform(key, (3, BEADS_DEV * DEVICES), jnp.float32)
    corners = []
    for corner in range(8):
        weight_x = fraction[0] if corner >> 2 & 1 else 1.0 - fraction[0]
        weight_y = fraction[1] if corner >> 1 & 1 else 1.0 - fraction[1]
        weight_z = fraction[2] if corner & 1 else 1.0 - fraction[2]
        corners.append(weight_x * weight_y * weight_z)
    return jnp.stack(corners)


def draw_slot_cell(key, part):
    rows = DEVICES * PLANE
    local_x = jax.random.randint(jax.random.fold_in(key, 7070), (rows, SLOTS), 0, CX)
    local_y = jax.random.randint(jax.random.fold_in(key, 7171), (rows, SLOTS), 0, CY)
    local_z = jax.random.randint(jax.random.fold_in(key, 7272), (rows, SLOTS), 0, CZ)
    return jnp.stack([local_x, local_y, local_z]).astype(jnp.int32)


def draw_corner_slot(key, part):

    def one_device(device):
        device_key = jax.random.fold_in(jax.random.fold_in(key, 6060), device)
        key_counts, key_picks = jax.random.split(device_key)
        plane_z = device % N_BZ
        home = device // N_BZ
        crowded = jax.random.randint(jax.random.fold_in(jax.random.fold_in(key, 6161), plane_z), (), 0, PLANE)
        counts = jax.random.randint(key_counts, (PLANE,), SLOTS // 8, SLOTS // 2 + 1)
        brick_index = jnp.arange(PLANE, dtype=jnp.int32)
        counts = jnp.where((brick_index == home) | (brick_index == crowded), SLOTS, counts).astype(jnp.int32)
        running = jnp.cumsum(counts).astype(jnp.int32)
        picks = jax.random.randint(key_picks, (8, BEADS_DEV), 0, running[-1])
        target = jnp.searchsorted(running, picks, side='right').astype(jnp.int32)
        within = picks - (running[target] - counts[target])
        return jnp.stack([target, within]).astype(jnp.int32)
    blocks = jax.vmap(one_device)(jnp.arange(DEVICES, dtype=jnp.int32))
    return jnp.transpose(blocks, (1, 2, 0, 3)).reshape(2, 8, -1).astype(jnp.int32)


def set_ends(entries, own_key, smallest, largest):
    extent = entries.shape
    index_at = [jax.random.randint(jax.random.fold_in(own_key, axis), (), 0, extent[axis]) for axis in range(len(extent))]
    entries = entries.at[tuple(index_at)].set(smallest)
    longest = extent.index(max(extent))
    index_at[longest] = (index_at[longest] + 1) % extent[longest]
    return entries.at[tuple(index_at)].set(largest)


def steps_of(rng, shape, cuts, least, top_value):
    def one(dim, shards_of):
        draws = jax.random.uniform(jax.random.fold_in(jax.random.fold_in(rng, 6), dim), (shards_of,), jnp.float32, least / len(cuts), top_value / len(cuts))
        return jnp.repeat(jnp.exp(draws), shape[dim] // shards_of).reshape((-1,) + (1,) * (len(shape) - dim - 1))

    loudness = one(*cuts[0])
    for cut in cuts[1:]:
        loudness = loudness * one(*cut)
    return loudness


def scatter_about(rng, shape, spread, reach, cuts=(), kind=jnp.bfloat16):
    array = spread * jax.random.normal(rng, shape, jnp.float32)
    if cuts:
        array = array * steps_of(rng, shape, cuts, -0.22, 0.18)
    return jnp.clip(array, -reach, reach).astype(kind)


def setup_inputs(seed: int = 0) -> dict:
    splits = jax.random.split(jax.random.key(seed), 8)
    return {
        "positions": draw_positions(jax.random.fold_in(splits[7], 71), 0),
        "velocities": scatter_about(splits[1], (3, BEADS), 1.0, 6.0, ((1, 256),), jnp.float32),
        "species": set_ends((jax.random.randint(splits[2], (BEADS,), 0, 2) < 1).astype(jnp.int32), jax.random.fold_in(splits[2], 1), 0, 1),
        "corner_slot": draw_corner_slot(jax.random.fold_in(splits[7], 71), 0),
        "corner_weight": draw_corner_weight(jax.random.fold_in(splits[7], 71), 0),
        "slot_cell": draw_slot_cell(jax.random.fold_in(splits[7], 71), 0),
        "bond_pairs": draw_bond_pairs(jax.random.fold_in(splits[7], 71), 0),
    }


spread_cells = 1.0
mixing = 10.0
stiffness = 5.0
time_step = 0.1
bond_length = 1.0


def gauss_taps():
    raw_list = [math.exp(-0.5 * (offset - REACH) ** 2 / spread_cells ** 2) for offset in range(2 * REACH + 1)]
    tap_total = sum(raw_list)
    return [entry / tap_total for entry in raw_list]


def smooth_periodic(field, axis):
    taps = gauss_taps()
    result = jnp.zeros_like(field)
    for offset in range(2 * REACH + 1):
        result = result + taps[offset] * jnp.roll(field, REACH - offset, axis=axis)
    return result


def constrain(anchor, moved, first, second):
    separation = anchor[:, first] - anchor[:, second]
    for repeat in range(SWEEPS):
        stretch = moved[:, first] - moved[:, second]
        excess = jnp.sum(stretch * stretch, axis=0) - bond_length * bond_length
        intersection = jnp.maximum(jnp.sum(stretch * separation, axis=0), 0.5 * bond_length * bond_length)
        factor = excess / (4.0 * intersection)
        shifted = factor * separation
        moved = moved.at[:, first].add(-shifted).at[:, second].add(shifted)
    return moved


def reference(positions, velocities, species, corner_slot, corner_weight, slot_cell, bond_pairs):
    bead_index = jnp.arange(BEADS, dtype=jnp.int32)
    owner = bead_index // BEADS_DEV
    plane_src = owner // N_BZ
    plane_z = owner % N_BZ
    target = corner_slot[0]
    within = corner_slot[1]
    row_index = ((target * N_BZ + plane_z[None, :]) * PLANE + plane_src[None, :]).astype(jnp.int32)
    local_x = slot_cell[0][row_index, within]
    local_y = slot_cell[1][row_index, within]
    local_z = slot_cell[2][row_index, within]
    cell_x = (target // N_BY) * CX + local_x
    cell_y = (target % N_BY) * CY + local_y
    cell_z = plane_z[None, :] * CZ + local_z
    global_cell = ((cell_x * NY + cell_y) * NZ + cell_z).astype(jnp.int32)
    is_lipid = (species == 0)[None, :]
    weight_a = jnp.where(is_lipid, corner_weight, 0.0)
    weight_b = jnp.where(is_lipid, 0.0, corner_weight)
    density = jnp.zeros((2, NX * NY * NZ), jnp.float32)
    density = density.at[0, global_cell.reshape(-1)].add(weight_a.reshape(-1))
    density = density.at[1, global_cell.reshape(-1)].add(weight_b.reshape(-1))
    density = density * (CX * CY * CZ / BEADS_DEV)
    filtered = density.reshape(2, NX, NY, NZ)
    for axis in (1, 2, 3):
        filtered = smooth_periodic(filtered, axis)
    combined = filtered[0] + filtered[1]
    potential = jnp.stack([mixing * filtered[1] + stiffness * combined, mixing * filtered[0] + stiffness * combined])
    components = []
    for axis in (1, 2, 3):
        slope = (jnp.roll(potential, -1, axis=axis) - jnp.roll(potential, 1, axis=axis)) * 0.5
        table = slope.reshape(2, -1)
        picked = jnp.where(is_lipid, table[0][global_cell], table[1][global_cell])
        components.append(-jnp.sum(corner_weight * picked, axis=0))
    force = jnp.stack(components)
    half = velocities + 0.5 * time_step * force
    moved = positions + time_step * half
    bond_owner = jnp.arange(BONDS, dtype=jnp.int32) // BONDS_DEV
    first = (bond_pairs[0] + bond_owner * BEADS_DEV).astype(jnp.int32)
    second = (bond_pairs[1] + bond_owner * BEADS_DEV).astype(jnp.int32)
    moved = constrain(positions, moved, first, second)
    new_velocities = (moved - positions) / time_step
    return moved, new_velocities, filtered
```

```python
import functools
import math

import jax
import jax.numpy as jnp
import numpy as np
from jax import lax
from jax.experimental import pallas as pl
from jax.experimental.pallas import tpu as pltpu
from jax.sharding import PartitionSpec as P

CX = 16
CY = 64
CZ = 64
BEADS_DEV = 4096
REACH = 3
SWEEPS = 4
SLOTS = 256
PLANE = 64
BONDS_DEV = 3840
OWNERS = ("bx", "by", "bz")
PLANE_AXES = ("bx", "by")

spread_cells = 1.0
mixing = 10.0
stiffness = 5.0
time_step = 0.1

F32 = jnp.float32
BF16 = jnp.bfloat16
NT = (((1,), (1,)), ((), ()))
NN = (((1,), (0,)), ((), ()))


def gauss_taps():
    raw_list = [
        math.exp(-0.5 * (offset - REACH) ** 2 / spread_cells**2) for offset in range(2 * REACH + 1)
    ]
    tap_total = sum(raw_list)
    return [entry / tap_total for entry in raw_list]


def mm(a, b, dims=NN):
    return lax.dot_general(a, b, dims, preferred_element_type=F32)


def two(x):
    hi = x.astype(BF16)
    return hi, (x - hi.astype(F32)).astype(BF16)


def three(x):
    hi = x.astype(BF16)
    rest = x - hi.astype(F32)
    mid = rest.astype(BF16)
    return hi, mid, (rest - mid.astype(F32)).astype(BF16)


def rows_iota(rows, n, dtype=BF16):
    return lax.broadcasted_iota(jnp.int32, (rows, n), 0).astype(F32).astype(dtype)


def onehot(index, rows):
    return jnp.where(
        rows_iota(rows, index.shape[1]) == index.astype(F32).astype(BF16),
        jnp.ones((), BF16),
        jnp.zeros((), BF16),
    )


def weighted(index, rows, value):
    return jnp.where(
        rows_iota(rows, index.shape[1]) == index.astype(F32).astype(BF16),
        value,
        jnp.zeros((), BF16),
    )


def pick(index, rows, values):
    n = index.shape[1]
    mask = lax.broadcasted_iota(jnp.int32, (rows, n), 0) == index
    return [
        jnp.sum(jnp.where(mask, values[g * rows : (g + 1) * rows], 0.0), axis=0, keepdims=True)
        for g in range(values.shape[0] // rows)
    ]


PACK_CHUNK = 1024


def pack_kernel(slot_ref, weight_ref, species_ref, out_ref, acc_ref):
    acc_ref[...] = jnp.zeros_like(acc_ref)

    def body(step, carry):
        c = step % 8
        cols = pl.ds(pl.multiple_of((step // 8) * PACK_CHUNK, PACK_CHUNK), PACK_CHUNK)
        brick = slot_ref[0, pl.ds(c, 1), cols]
        slot = slot_ref[1, pl.ds(c, 1), cols]
        kd = brick + PLANE * species_ref[:, cols]
        hi, lo = two(weight_ref[pl.ds(c, 1), cols])
        left = jnp.concatenate([weighted(kd, 2 * PLANE, hi), weighted(kd, 2 * PLANE, lo)], axis=0)
        acc_ref[...] += mm(left, onehot(slot, SLOTS), NT)
        return carry

    lax.fori_loop(0, 8 * BEADS_DEV // PACK_CHUNK, body, 0)
    total = acc_ref[: 2 * PLANE] + acc_ref[2 * PLANE :]
    out_ref[:, :SLOTS] = total[:PLANE]
    out_ref[:, SLOTS:] = total[PLANE:]


SPREAD_ROWS = 8


def onehot_xy(x, y):
    oy = onehot(y, CY)
    xb = x.astype(F32).astype(BF16)
    zero = jnp.zeros((), BF16)
    blocks = []
    for i in range(CX):
        blocks.append(jnp.where(xb == jnp.asarray(i, BF16), oy, zero))
    return jnp.concatenate(blocks, axis=0)


def spread_kernel(recv_ref, cell_ref, out_ref, xy_ref, z_ref, acc_ref):
    acc_ref[...] = jnp.zeros_like(acc_ref)

    def body(step, carry):
        for i in range(SPREAD_ROWS):
            p = step * SPREAD_ROWS + i
            x, y, z = (cell_ref[a, pl.ds(p, 1), :] for a in range(3))
            cols = slice(i * SLOTS, (i + 1) * SLOTS)
            xy_ref[:, cols] = onehot_xy(x, y)
            for k in range(2):
                hi, lo = two(recv_ref[pl.ds(p, 1), k * SLOTS : (k + 1) * SLOTS])
                z_ref[k * CZ : (k + 1) * CZ, cols] = weighted(z, CZ, hi)
                z_ref[(2 + k) * CZ : (3 + k) * CZ, cols] = weighted(z, CZ, lo)
        acc_ref[...] += mm(xy_ref[...], z_ref[...], NT)
        return carry

    lax.fori_loop(0, PLANE // SPREAD_ROWS, body, 0)
    total = (acc_ref[:, : 2 * CZ] + acc_ref[:, 2 * CZ :]) * (CX * CY * CZ / BEADS_DEV)
    out_ref[...] = total.reshape(CX, CY, 2 * CZ)


def filter_x_kernel(left_ref, own_ref, right_ref, out_ref, head_ref, tail_ref, ext_ref):
    taps = gauss_taps()
    w = REACH + 1
    ext_ref[:w] = left_ref[...]
    ext_ref[w : w + CX] = own_ref[...]
    ext_ref[w + CX :] = right_ref[...]

    def body(i, carry):
        total = taps[0] * ext_ref[i]
        for j in range(1, 2 * REACH + 1):
            total = total + taps[j] * ext_ref[i + j]
        out_ref[i] = total
        head_ref[i] = total[:w]
        tail_ref[i] = total[CY - w :]
        return carry

    lax.fori_loop(0, CX + 2, body, 0)


YP = 72


def filter_y_kernel(left_ref, own_ref, right_ref, out_ref, edge_ref, ext_ref):
    taps = gauss_taps()
    w = REACH + 1
    span = CY + 2
    ext_ref[:, :w] = left_ref[...]
    ext_ref[:, w : w + CY] = own_ref[...]
    ext_ref[:, w + CY :] = right_ref[...]
    row = lax.broadcasted_iota(jnp.int32, (16, 2 * CZ), 0)
    lane = lax.broadcasted_iota(jnp.int32, (16, 2 * CZ), 1)
    wanted = ((row % 8) // w) * CZ + (row // 8) * (CZ - w) + row % w
    select = jnp.where(lane == wanted, 1.0, 0.0).astype(BF16)

    def body(i, carry):
        total = taps[0] * ext_ref[i, :span]
        for j in range(1, 2 * REACH + 1):
            total = total + taps[j] * ext_ref[i, j : j + span]
        full = jnp.concatenate([total, jnp.zeros((YP - span, 2 * CZ), F32)], axis=0)
        out_ref[i] = full
        hi, mid, lo = three(full)
        edge_ref[i] = mm(select, hi, NT) + mm(select, mid, NT) + mm(select, lo, NT)
        return carry

    lax.fori_loop(0, CX + 2, body, 0)


def z_operators():
    taps = gauss_taps()
    w = REACH + 1
    smooth = np.zeros((CZ + 2 * w, CZ))
    slope = np.zeros((CZ + 2 * w, CZ))
    for z in range(CZ):
        for j in range(2 * REACH + 1):
            smooth[z + w + j - REACH, z] += taps[j]
            slope[z + w + 1 + j - REACH, z] += 0.5 * taps[j]
            slope[z + w - 1 + j - REACH, z] -= 0.5 * taps[j]
    mix = np.array([[stiffness, mixing + stiffness], [mixing + stiffness, stiffness]])
    full = np.concatenate(
        [np.kron(np.eye(2), smooth), np.kron(mix.T, smooth), np.kron(mix.T, slope)], axis=1
    ).reshape(2, CZ + 2 * w, 6 * CZ)
    own = full[:, w : w + CZ].reshape(2 * CZ, 6 * CZ)
    halo = np.concatenate(
        [full[:, :w].reshape(2 * w, 6 * CZ), full[:, w + CZ :].reshape(2 * w, 6 * CZ)]
    )
    return own.astype(np.float32), halo.astype(np.float32)


def mm3(a, b_hi, b_lo):
    a_hi, a_lo = two(a)
    return mm(a_hi, b_hi) + (mm(a_hi, b_lo) + mm(a_lo, b_hi))


GATHER_ROWS = 2


def slopes_kernel(
    own_ref, left_ref, right_ref, op_ref, hop_ref, smooth_ref, table_ref, p_ref, pz_ref
):
    op_hi, op_lo = two(op_ref[...])
    hop_hi, hop_lo = two(hop_ref[...])
    wide = 2 * CZ

    def filter_z(i, carry):
        halo = jnp.concatenate([left_ref[i], right_ref[i]], axis=0).T
        both = mm3(own_ref[i], op_hi, op_lo) + mm3(halo, hop_hi, hop_lo)
        p_ref[i] = both[:, wide : 2 * wide]
        pz_ref[i] = both[:, 2 * wide :]

        @pl.when((i > 0) & (i <= CX))
        def _():
            for k in range(2):
                smooth_ref[k, i - 1] = both[1 : CY + 1, k * CZ : (k + 1) * CZ]

        return carry

    lax.fori_loop(0, CX + 2, filter_z, 0)

    for i in range(0, CX, 2):
        parts = []
        for q in (i + 1, i + 2):
            sx = (p_ref[q + 1, 1 : CY + 1] - p_ref[q - 1, 1 : CY + 1]) * 0.5
            sy = (p_ref[q, 2 : CY + 2] - p_ref[q, :CY]) * 0.5
            sz = pz_ref[q, 1 : CY + 1]
            parts.append((sx, sy, sz))
        cols = slice(i * CY, (i + 2) * CY)
        for a in range(3):
            hi, lo = two(jnp.concatenate([parts[0][a], parts[1][a]], axis=0).T)
            table_ref[a * wide : (a + 1) * wide, cols] = hi
            table_ref[(3 + a) * wide : (4 + a) * wide, cols] = lo


def lookup_kernel(table_ref, cell_ref, out_ref):
    def body(step, carry):
        p0 = step * GATHER_ROWS
        xyz = [
            jnp.concatenate(
                [cell_ref[a, pl.ds(p0 + i, 1), :] for i in range(GATHER_ROWS)], axis=1
            )
            for a in range(3)
        ]
        both = mm(table_ref[...], onehot_xy(xyz[0], xyz[1]))
        half = 6 * CZ
        found = pick(xyz[2], CZ, both[:half] + both[half:])
        for g in range(6):
            for i in range(GATHER_ROWS):
                out_ref[g, pl.ds(p0 + i, 1), :] = found[g][:, i * SLOTS : (i + 1) * SLOTS]
        return carry

    lax.fori_loop(0, PLANE // GATHER_ROWS, body, 0)


HALF = BONDS_DEV
ENDS = 2 * BONDS_DEV


def to_rows(x):
    return jnp.concatenate([x[:, i : i + 128] for i in range(0, x.shape[1], 128)], axis=0)


def to_line(x):
    return jnp.concatenate([x[i : i + 1] for i in range(x.shape[0])], axis=1)


def bonds_kernel(pairs_ref, positions_ref, out_ref, oh_ref):
    pairs = jnp.concatenate([pairs_ref[0:1], pairs_ref[1:2]], axis=1)
    hi_index = pairs >> 7
    oh_ref[...] = onehot(pairs & 127, 128)
    number = lax.broadcasted_iota(jnp.int32, (1, HALF), 1)
    number = jnp.concatenate([number, number], axis=1)
    sign = jnp.where(lax.broadcasted_iota(jnp.int32, (1, ENDS), 1) < HALF, 1.0, -1.0)
    left = jnp.concatenate(
        [
            weighted(hi_index, 32, v.astype(F32).astype(BF16))
            for v in (number >> 6, number & 63, sign)
        ],
        axis=0,
    )
    sums = mm(left, oh_ref[...], NT).astype(BF16)
    high, low, signs = pick(hi_index, 32, mm(sums, oh_ref[...]))
    other = 64.0 * high + low - number.astype(F32)
    other_sign = signs - sign
    parts = [three(to_rows(positions_ref[a : a + 1])) for a in range(3)]
    table = [jnp.concatenate([parts[a][q] for a in range(3)], axis=0) for q in range(3)]
    oh = oh_ref[...]
    ends = pick(hi_index, 32, mm(table[0], oh) + mm(table[1], oh) + mm(table[2], oh))
    for a in range(3):
        out_ref[a : a + 1] = ends[a][:, :HALF] - ends[a][:, HALF:]
    out_ref[3:4] = other[:, :HALF]
    out_ref[4:5] = other[:, HALF:]
    out_ref[5:6] = other_sign[:, :HALF]
    out_ref[6:7] = other_sign[:, HALF:]
    out_ref[7:8] = jnp.zeros((1, HALF), F32)


FORCE_CHUNK = 512


def force_kernel(
    table_ref, slot_ref, weight_ref, species_ref, pos_ref, vel_ref, delta_ref, hi_ref, lo_ref
):
    hi, lo = two(table_ref[...])
    hi_ref[...] = hi
    lo_ref[...] = lo
    wide = 2 * PLANE

    def body(step, carry):
        cols = pl.ds(pl.multiple_of(step * FORCE_CHUNK, FORCE_CHUNK), FORCE_CHUNK)
        species = species_ref[:, cols]
        force = [jnp.zeros((1, FORCE_CHUNK), F32)] * 3
        for c in range(8):
            oh = onehot(slot_ref[1, c : c + 1, cols], SLOTS)
            both = mm(hi_ref[...], oh) + mm(lo_ref[...], oh)
            found = pick(slot_ref[0, c : c + 1, cols] + PLANE * species, wide, both)
            weight = weight_ref[c : c + 1, cols]
            force = [force[a] - weight * found[a] for a in range(3)]
        for a in range(3):
            half = vel_ref[a : a + 1, cols] + 0.5 * time_step * force[a]
            delta_ref[a : a + 1, cols] = time_step * half
        return carry

    lax.fori_loop(0, BEADS_DEV // FORCE_CHUNK, body, 0)


def constrain_kernel(pairs_ref, bonds_ref, delta_ref, pos_ref, newpos_ref, newvel_ref, oh_ref, nb_ref):
    pairs = jnp.concatenate([pairs_ref[0:1], pairs_ref[1:2]], axis=1)
    hi_index = pairs >> 7
    oh_ref[...] = onehot(pairs & 127, 128)
    r = [bonds_ref[a : a + 1] for a in range(3)]
    other = jnp.concatenate([bonds_ref[3:4], bonds_ref[4:5]], axis=1).astype(jnp.int32)
    sign = [bonds_ref[5:6], bonds_ref[6:7]]
    other_hi = other >> 7
    nb_ref[...] = onehot(other & 127, 128)
    delta = [delta_ref[a : a + 1] for a in range(3)]
    parts = [two(to_rows(d)) for d in delta]
    table = [jnp.concatenate([parts[a][q] for a in range(3)], axis=0) for q in range(2)]
    ends = pick(hi_index, 32, mm(table[0], oh_ref[...]) + mm(table[1], oh_ref[...]))
    v = [r[a] + (ends[a][:, :HALF] - ends[a][:, HALF:]) for a in range(3)]
    total = [jnp.zeros((1, HALF), F32)] * 3
    for sweep in range(SWEEPS):
        vv = v[0] * v[0] + v[1] * v[1] + v[2] * v[2]
        vr = v[0] * r[0] + v[1] * r[1] + v[2] * r[2]
        g = (vv - 1.0) / (4.0 * jnp.maximum(vr, 0.5))
        shift = [g * r[a] for a in range(3)]
        total = [total[a] + shift[a] for a in range(3)]
        if sweep + 1 == SWEEPS:
            break
        pad = jnp.zeros((2, 128), F32)
        parts = [two(jnp.concatenate([to_rows(s), pad], axis=0)) for s in shift]
        table = [jnp.concatenate([parts[a][q] for a in range(3)], axis=0) for q in range(2)]
        near = pick(other_hi, 32, mm(table[0], nb_ref[...]) + mm(table[1], nb_ref[...]))
        v = [
            v[a] - 2.0 * shift[a] - sign[0] * near[a][:, :HALF] + sign[1] * near[a][:, HALF:]
            for a in range(3)
        ]
    rows = []
    for a in range(3):
        both = jnp.concatenate([total[a], -total[a]], axis=1)
        rows += [weighted(hi_index, 32, q) for q in two(both)]
    moved = mm(jnp.concatenate(rows, axis=0), oh_ref[...], NT)
    for a in range(3):
        q = to_line(moved[64 * a : 64 * a + 32] + moved[64 * a + 32 : 64 * a + 64])
        change = delta[a] - q
        newpos_ref[a : a + 1] = pos_ref[a : a + 1] + change
        newvel_ref[a : a + 1] = change / time_step


def call(kernel, out_shapes, scratch, name):
    many = isinstance(out_shapes, list)
    shapes = [jax.ShapeDtypeStruct(s, d) for s, d in (out_shapes if many else [out_shapes])]
    return pl.pallas_call(
        kernel,
        out_shape=shapes if many else shapes[0],
        scratch_shapes=scratch,
        compiler_params=pltpu.CompilerParams(vmem_limit_bytes=60 * 1024 * 1024),
        name=name,
    )


def neighbours(head, tail, axis):
    count = lax.axis_size(axis)
    up = [(i, (i + 1) % count) for i in range(count)]
    down = [((i + 1) % count, i) for i in range(count)]
    return lax.ppermute(tail, axis, up), lax.ppermute(head, axis, down)


def on_device(positions, velocities, species, corner_slot, corner_weight, slot_cell, bond_pairs):
    w = REACH + 1
    wide = 2 * CZ
    species = species[None, :]
    packets = call(pack_kernel, ((PLANE, 2 * SLOTS), F32), [pltpu.VMEM((256, SLOTS), F32)], "pack")(
        corner_slot, corner_weight, species
    )
    bonds = call(
        bonds_kernel, ((8, BONDS_DEV), F32), [pltpu.VMEM((128, ENDS), BF16)], "bonds"
    )(bond_pairs, positions)
    received = lax.all_to_all(packets, PLANE_AXES, split_axis=0, concat_axis=0, tiled=True)
    density = call(
        spread_kernel,
        ((CX, CY, wide), F32),
        [
            pltpu.VMEM((CX * CY, SPREAD_ROWS * SLOTS), BF16),
            pltpu.VMEM((4 * CZ, SPREAD_ROWS * SLOTS), BF16),
            pltpu.VMEM((CX * CY, 4 * CZ), F32),
        ],
        "spread",
    )(received, slot_cell)
    left, right = neighbours(density[:w], density[CX - w :], "bx")
    along_x, head, tail = call(
        filter_x_kernel,
        [((CX + 2, CY, wide), F32), ((CX + 2, w, wide), F32), ((CX + 2, w, wide), F32)],
        [pltpu.VMEM((CX + 2 * w, CY, wide), F32)],
        "filter_x",
    )(left, density, right)
    left, right = neighbours(head, tail, "by")
    along_y, edge = call(
        filter_y_kernel,
        [((CX + 2, YP, wide), F32), ((CX + 2, 16, YP), F32)],
        [pltpu.VMEM((CX + 2, CY + 2 * w, wide), F32)],
        "filter_y",
    )(left, along_x, right)
    left, right = neighbours(edge[:, :8], edge[:, 8:], "bz")
    own_op, halo_op = z_operators()
    smoothed, table = call(
        slopes_kernel,
        [((2, CX, CY, CZ), F32), ((6 * wide, CX * CY), BF16)],
        [pltpu.VMEM((CX + 2, YP, wide), F32), pltpu.VMEM((CX + 2, YP, wide), F32)],
        "slopes",
    )(along_y, left, right, jnp.asarray(own_op), jnp.asarray(halo_op))
    outgoing = call(lookup_kernel, ((6, PLANE, SLOTS), F32), [], "lookup")(table, slot_cell)
    returned = lax.all_to_all(outgoing, PLANE_AXES, split_axis=1, concat_axis=1, tiled=True)
    delta = call(
        force_kernel,
        ((3, BEADS_DEV), F32),
        [pltpu.VMEM((6 * PLANE, SLOTS), BF16), pltpu.VMEM((6 * PLANE, SLOTS), BF16)],
        "force",
    )(returned.reshape(6 * PLANE, SLOTS), corner_slot, corner_weight, species, positions, velocities)
    moved, new_velocities = call(
        constrain_kernel,
        [((3, BEADS_DEV), F32), ((3, BEADS_DEV), F32)],
        [pltpu.VMEM((128, ENDS), BF16), pltpu.VMEM((128, ENDS), BF16)],
        "constrain",
    )(bond_pairs, bonds, delta, positions)
    return (moved, new_velocities, smoothed)


def solution(mesh):
    placed = (
        P(None, OWNERS),
        P(None, OWNERS),
        P(OWNERS),
        P(None, None, OWNERS),
        P(None, OWNERS),
        P(None, OWNERS, None),
        P(None, OWNERS),
    )
    return jax.shard_map(
        on_device,
        mesh=mesh,
        in_specs=placed,
        out_specs=(P(None, OWNERS), P(None, OWNERS), P(None, "bx", "by", "bz")),
        check_vma=False,
    )
```

```python
import functools
import math

import jax
import jax.numpy as jnp
import numpy as np
from jax import lax
from jax.experimental import pallas as pl
from jax.experimental.pallas import tpu as pltpu
from jax.sharding import PartitionSpec as P

CX = 16
CY = 64
CZ = 64
BEADS_DEV = 4096
REACH = 3
SWEEPS = 4
SLOTS = 256
PLANE = 64
BONDS_DEV = 3840
OWNERS = ("bx", "by", "bz")
N_BY = 8
MESH = pl.DeviceIdType.MESH
PACK_CHUNK = 1024
SPREAD_ROWS = 8
GATHER_ROWS = 2
FORCE_CHUNK = 512
YP = 72
W = REACH + 1
WIDE = 2 * CZ
HALF = BONDS_DEV
ENDS = 2 * BONDS_DEV

spread_cells = 1.0
mixing = 10.0
stiffness = 5.0
time_step = 0.1

F32 = jnp.float32
BF16 = jnp.bfloat16
NT = (((1,), (1,)), ((), ()))
NN = (((1,), (0,)), ((), ()))


def gauss_taps():
    raw_list = [
        math.exp(-0.5 * (offset - REACH) ** 2 / spread_cells**2) for offset in range(2 * REACH + 1)
    ]
    tap_total = sum(raw_list)
    return [entry / tap_total for entry in raw_list]


def mm(a, b, dims=NN):
    return lax.dot_general(a, b, dims, preferred_element_type=F32)


def two(x):
    hi = x.astype(BF16)
    return hi, (x - hi.astype(F32)).astype(BF16)


def three(x):
    hi = x.astype(BF16)
    rest = x - hi.astype(F32)
    mid = rest.astype(BF16)
    return hi, mid, (rest - mid.astype(F32)).astype(BF16)


def rows_iota(rows, n, dtype=BF16):
    return lax.broadcasted_iota(jnp.int32, (rows, n), 0).astype(F32).astype(dtype)


def onehot(index, rows):
    return jnp.where(
        rows_iota(rows, index.shape[1]) == index.astype(F32).astype(BF16),
        jnp.ones((), BF16),
        jnp.zeros((), BF16),
    )


def weighted(index, rows, value):
    return jnp.where(
        rows_iota(rows, index.shape[1]) == index.astype(F32).astype(BF16),
        value,
        jnp.zeros((), BF16),
    )


def pick(index, rows, values):
    n = index.shape[1]
    mask = lax.broadcasted_iota(jnp.int32, (rows, n), 0) == index
    return [
        jnp.sum(jnp.where(mask, values[g * rows : (g + 1) * rows], 0.0), axis=0, keepdims=True)
        for g in range(values.shape[0] // rows)
    ]


def onehot_xy(x, y):
    oy = onehot(y, CY)
    xb = x.astype(F32).astype(BF16)
    zero = jnp.zeros((), BF16)
    blocks = []
    for i in range(CX):
        blocks.append(jnp.where(xb == jnp.asarray(i, BF16), oy, zero))
    return jnp.concatenate(blocks, axis=0)


def z_operators():
    taps = gauss_taps()
    w = REACH + 1
    smooth = np.zeros((CZ + 2 * w, CZ))
    slope = np.zeros((CZ + 2 * w, CZ))
    for z in range(CZ):
        for j in range(2 * REACH + 1):
            smooth[z + w + j - REACH, z] += taps[j]
            slope[z + w + 1 + j - REACH, z] += 0.5 * taps[j]
            slope[z + w - 1 + j - REACH, z] -= 0.5 * taps[j]
    mix = np.array([[stiffness, mixing + stiffness], [mixing + stiffness, stiffness]])
    full = np.concatenate(
        [np.kron(np.eye(2), smooth), np.kron(mix.T, smooth), np.kron(mix.T, slope)], axis=1
    ).reshape(2, CZ + 2 * w, 6 * CZ)
    own = full[:, w : w + CZ].reshape(2 * CZ, 6 * CZ)
    halo = np.concatenate(
        [full[:, :w].reshape(2 * w, 6 * CZ), full[:, w + CZ :].reshape(2 * w, 6 * CZ)]
    )
    return own.astype(np.float32), halo.astype(np.float32)


def mm3(a, b_hi, b_lo):
    a_hi, a_lo = two(a)
    return mm(a_hi, b_hi) + (mm(a_hi, b_lo) + mm(a_lo, b_hi))


def to_rows(x):
    return jnp.concatenate([x[:, i : i + 128] for i in range(0, x.shape[1], 128)], axis=0)


def to_line(x):
    return jnp.concatenate([x[i : i + 1] for i in range(x.shape[0])], axis=1)


def pack(slot_ref, weight_ref, species_ref, send_ref, acc_ref):
    acc_ref[...] = jnp.zeros_like(acc_ref)

    def body(step, carry):
        c = step % 8
        cols = pl.ds(pl.multiple_of((step // 8) * PACK_CHUNK, PACK_CHUNK), PACK_CHUNK)
        brick = slot_ref[0, pl.ds(c, 1), cols]
        slot = slot_ref[1, pl.ds(c, 1), cols]
        kd = brick + PLANE * species_ref[:, cols]
        hi, lo = two(weight_ref[pl.ds(c, 1), cols])
        left = jnp.concatenate([weighted(kd, 2 * PLANE, hi), weighted(kd, 2 * PLANE, lo)], axis=0)
        acc_ref[...] += mm(left, onehot(slot, SLOTS), NT)
        return carry

    lax.fori_loop(0, 8 * BEADS_DEV // PACK_CHUNK, body, 0)
    total = acc_ref[: 2 * PLANE] + acc_ref[2 * PLANE :]
    send_ref[:, 0, :] = total[:PLANE]
    send_ref[:, 1, :] = total[PLANE:]


def spread(me, arrive, recv_ref, cell_ref, ext_ref, xy_ref, z_ref, acc_ref):
    acc_ref[...] = jnp.zeros_like(acc_ref)

    def body(step, carry):
        for i in range(SPREAD_ROWS):
            t = step * SPREAD_ROWS + i
            p = lax.rem(me - t + PLANE, PLANE)
            arrive(t, p)
            x, y, z = (cell_ref[a, pl.ds(p, 1), :] for a in range(3))
            cols = slice(i * SLOTS, (i + 1) * SLOTS)
            xy_ref[:, cols] = onehot_xy(x, y)
            for k in range(2):
                hi, lo = two(recv_ref[p, k : k + 1, :])
                z_ref[k * CZ : (k + 1) * CZ, cols] = weighted(z, CZ, hi)
                z_ref[(2 + k) * CZ : (3 + k) * CZ, cols] = weighted(z, CZ, lo)
        acc_ref[...] += mm(xy_ref[...], z_ref[...], NT)
        return carry

    lax.fori_loop(0, PLANE // SPREAD_ROWS, body, 0)
    total = (acc_ref[:, :WIDE] + acc_ref[:, WIDE:]) * (CX * CY * CZ / BEADS_DEV)
    ext_ref[W : W + CX] = total.reshape(CX, CY, WIDE)


def filter_x(ext_ref, ey_ref, head_ref, tail_ref):
    taps = gauss_taps()

    def body(i, carry):
        total = taps[0] * ext_ref[i]
        for j in range(1, 2 * REACH + 1):
            total = total + taps[j] * ext_ref[i + j]
        ey_ref[i, W : W + CY] = total
        head_ref[i] = total[:W]
        tail_ref[i] = total[CY - W :]
        return carry

    lax.fori_loop(0, CX + 2, body, 0)


def filter_y(left_ref, right_ref, ey_ref, ay_ref, head_ref, tail_ref):
    taps = gauss_taps()
    span = CY + 2
    row = lax.broadcasted_iota(jnp.int32, (16, WIDE), 0)
    lane = lax.broadcasted_iota(jnp.int32, (16, WIDE), 1)
    wanted = ((row % 8) // W) * CZ + (row // 8) * (CZ - W) + row % W
    select = jnp.where(lane == wanted, 1.0, 0.0).astype(BF16)
    ey_ref[:, :W] = left_ref[...]
    ey_ref[:, W + CY :] = right_ref[...]

    def body(i, carry):
        total = taps[0] * ey_ref[i, :span]
        for j in range(1, 2 * REACH + 1):
            total = total + taps[j] * ey_ref[i, j : j + span]
        full = jnp.concatenate([total, jnp.zeros((YP - span, WIDE), F32)], axis=0)
        ay_ref[i] = full
        hi, mid, lo = three(full)
        edge = mm(select, hi, NT) + mm(select, mid, NT) + mm(select, lo, NT)
        head_ref[i] = edge[:8]
        tail_ref[i] = edge[8:]
        return carry

    lax.fori_loop(0, CX + 2, body, 0)


def slopes(left_ref, right_ref, op_ref, hop_ref, ay_ref, smooth_ref, table_ref, p_ref, pz_ref):
    op_hi, op_lo = two(op_ref[...])
    hop_hi, hop_lo = two(hop_ref[...])

    def filter_z(i, carry):
        halo = jnp.concatenate([left_ref[i], right_ref[i]], axis=0).T
        both = mm3(ay_ref[i], op_hi, op_lo) + mm3(halo, hop_hi, hop_lo)
        p_ref[i] = both[:, WIDE : 2 * WIDE]
        pz_ref[i] = both[:, 2 * WIDE :]

        @pl.when((i > 0) & (i <= CX))
        def _():
            for k in range(2):
                smooth_ref[k, i - 1] = both[1 : CY + 1, k * CZ : (k + 1) * CZ]

        return carry

    lax.fori_loop(0, CX + 2, filter_z, 0)

    for i in range(0, CX, 2):
        parts = []
        for q in (i + 1, i + 2):
            sx = (p_ref[q + 1, 1 : CY + 1] - p_ref[q - 1, 1 : CY + 1]) * 0.5
            sy = (p_ref[q, 2 : CY + 2] - p_ref[q, :CY]) * 0.5
            sz = pz_ref[q, 1 : CY + 1]
            parts.append((sx, sy, sz))
        cols = slice(i * CY, (i + 2) * CY)
        for a in range(3):
            hi, lo = two(jnp.concatenate([parts[0][a], parts[1][a]], axis=0).T)
            table_ref[a * WIDE : (a + 1) * WIDE, cols] = hi
            table_ref[(3 + a) * WIDE : (4 + a) * WIDE, cols] = lo


def lookup(me, leave, table_ref, cell_ref, send_ref):
    def body(step, carry):
        owners = [lax.rem(me + 1 + step * GATHER_ROWS + i, PLANE) for i in range(GATHER_ROWS)]
        xyz = [
            jnp.concatenate([cell_ref[a, pl.ds(p, 1), :] for p in owners], axis=1)
            for a in range(3)
        ]
        both = mm(table_ref[...], onehot_xy(xyz[0], xyz[1]))
        half = 6 * CZ
        found = pick(xyz[2], CZ, both[:half] + both[half:])
        for i, p in enumerate(owners):
            cols = slice(i * SLOTS, (i + 1) * SLOTS)
            send_ref[p] = jnp.concatenate([found[g][:, cols] for g in range(6)], axis=0)
        for p in owners:
            leave(p)
        return carry

    lax.fori_loop(0, PLANE // GATHER_ROWS, body, 0)


def forces(
    recv_ref, slot_ref, weight_ref, species_ref, vel_ref, delta_ref, hi_ref, lo_ref
):
    for g in range(6):
        hi, lo = two(recv_ref[:, g, :])
        hi_ref[g * PLANE : (g + 1) * PLANE] = hi
        lo_ref[g * PLANE : (g + 1) * PLANE] = lo
    wide = 2 * PLANE

    def body(step, carry):
        cols = pl.ds(pl.multiple_of(step * FORCE_CHUNK, FORCE_CHUNK), FORCE_CHUNK)
        species = species_ref[:, cols]
        force = [jnp.zeros((1, FORCE_CHUNK), F32)] * 3
        for c in range(8):
            oh = onehot(slot_ref[1, c : c + 1, cols], SLOTS)
            both = mm(hi_ref[...], oh) + mm(lo_ref[...], oh)
            found = pick(slot_ref[0, c : c + 1, cols] + PLANE * species, wide, both)
            weight = weight_ref[c : c + 1, cols]
            force = [force[a] - weight * found[a] for a in range(3)]
        for a in range(3):
            half = vel_ref[a : a + 1, cols] + 0.5 * time_step * force[a]
            delta_ref[a : a + 1, cols] = time_step * half
        return carry

    lax.fori_loop(0, BEADS_DEV // FORCE_CHUNK, body, 0)


def bonds(pairs_ref, positions_ref, out_ref, oh_ref):
    pairs = jnp.concatenate([pairs_ref[0:1], pairs_ref[1:2]], axis=1)
    hi_index = pairs >> 7
    oh_ref[...] = onehot(pairs & 127, 128)
    number = lax.broadcasted_iota(jnp.int32, (1, HALF), 1)
    number = jnp.concatenate([number, number], axis=1)
    sign = jnp.where(lax.broadcasted_iota(jnp.int32, (1, ENDS), 1) < HALF, 1.0, -1.0)
    left = jnp.concatenate(
        [
            weighted(hi_index, 32, v.astype(F32).astype(BF16))
            for v in (number >> 6, number & 63, sign)
        ],
        axis=0,
    )
    sums = mm(left, oh_ref[...], NT).astype(BF16)
    high, low, signs = pick(hi_index, 32, mm(sums, oh_ref[...]))
    other = 64.0 * high + low - number.astype(F32)
    other_sign = signs - sign
    parts = [three(to_rows(positions_ref[a : a + 1])) for a in range(3)]
    table = [jnp.concatenate([parts[a][q] for a in range(3)], axis=0) for q in range(3)]
    oh = oh_ref[...]
    ends = pick(hi_index, 32, mm(table[0], oh) + mm(table[1], oh) + mm(table[2], oh))
    for a in range(3):
        out_ref[a : a + 1] = ends[a][:, :HALF] - ends[a][:, HALF:]
    out_ref[3:4] = other[:, :HALF]
    out_ref[4:5] = other[:, HALF:]
    out_ref[5:6] = other_sign[:, :HALF]
    out_ref[6:7] = other_sign[:, HALF:]
    out_ref[7:8] = jnp.zeros((1, HALF), F32)


def constrain(pairs_ref, bonds_ref, delta_ref, pos_ref, newpos_ref, newvel_ref, oh_ref, nb_ref):
    pairs = jnp.concatenate([pairs_ref[0:1], pairs_ref[1:2]], axis=1)
    hi_index = pairs >> 7
    r = [bonds_ref[a : a + 1] for a in range(3)]
    other = jnp.concatenate([bonds_ref[3:4], bonds_ref[4:5]], axis=1).astype(jnp.int32)
    sign = [bonds_ref[5:6], bonds_ref[6:7]]
    other_hi = other >> 7
    nb_ref[...] = onehot(other & 127, 128)
    delta = [delta_ref[a : a + 1] for a in range(3)]
    parts = [two(to_rows(d)) for d in delta]
    table = [jnp.concatenate([parts[a][q] for a in range(3)], axis=0) for q in range(2)]
    ends = pick(hi_index, 32, mm(table[0], oh_ref[...]) + mm(table[1], oh_ref[...]))
    v = [r[a] + (ends[a][:, :HALF] - ends[a][:, HALF:]) for a in range(3)]
    total = [jnp.zeros((1, HALF), F32)] * 3
    for sweep in range(SWEEPS):
        vv = v[0] * v[0] + v[1] * v[1] + v[2] * v[2]
        vr = v[0] * r[0] + v[1] * r[1] + v[2] * r[2]
        g = (vv - 1.0) / (4.0 * jnp.maximum(vr, 0.5))
        shift = [g * r[a] for a in range(3)]
        total = [total[a] + shift[a] for a in range(3)]
        if sweep + 1 == SWEEPS:
            break
        pad = jnp.zeros((2, 128), F32)
        parts = [two(jnp.concatenate([to_rows(s), pad], axis=0)) for s in shift]
        table = [jnp.concatenate([parts[a][q] for a in range(3)], axis=0) for q in range(2)]
        near = pick(other_hi, 32, mm(table[0], nb_ref[...]) + mm(table[1], nb_ref[...]))
        v = [
            v[a] - 2.0 * shift[a] - sign[0] * near[a][:, :HALF] + sign[1] * near[a][:, HALF:]
            for a in range(3)
        ]
    rows = []
    for a in range(3):
        both = jnp.concatenate([total[a], -total[a]], axis=1)
        rows += [weighted(hi_index, 32, q) for q in two(both)]
    moved = mm(jnp.concatenate(rows, axis=0), oh_ref[...], NT)
    for a in range(3):
        q = to_line(moved[64 * a : 64 * a + 32] + moved[64 * a + 32 : 64 * a + 64])
        change = delta[a] - q
        newpos_ref[a : a + 1] = pos_ref[a : a + 1] + change
        newvel_ref[a : a + 1] = change / time_step


def step_kernel(
    slot_ref,
    weight_ref,
    species_ref,
    cell_ref,
    pairs_ref,
    pos_ref,
    vel_ref,
    op_ref,
    hop_ref,
    newpos_ref,
    newvel_ref,
    smooth_ref,
    acc1_ref,
    send1_ref,
    recv1_ref,
    xy_ref,
    z_ref,
    acc2_ref,
    ext_ref,
    ey_ref,
    yside_ref,
    ay_ref,
    zside_ref,
    p_ref,
    pz_ref,
    table_ref,
    send2_ref,
    recv2_ref,
    hi_ref,
    lo_ref,
    delta_ref,
    bonds_ref,
    oh_ref,
    nb_ref,
    out_sem,
    in_sem,
    back_out_sem,
    back_in_sem,
    side_out_sem,
    side_in_sem,
):
    bx, by, bz = (lax.axis_index(a) for a in OWNERS)
    me = bx * N_BY + by
    counts = [lax.axis_size(a) for a in OWNERS]

    def owner(p):
        return (p // N_BY, lax.rem(p, N_BY), bz)

    def shifted(axis, by_how):
        place = [bx, by, bz]
        place[axis] = lax.rem(place[axis] + by_how + counts[axis], counts[axis])
        return tuple(place)

    barrier = pltpu.get_barrier_semaphore()

    def greet(t, carry):
        p = lax.rem(me + t, PLANE)
        pl.semaphore_signal(barrier, inc=1, device_id=owner(p), device_id_type=MESH)
        return carry

    lax.fori_loop(1, PLANE, greet, 0)
    for by_how in (-1, 1):
        pl.semaphore_signal(barrier, inc=1, device_id=shifted(2, by_how), device_id_type=MESH)

    pack(slot_ref, weight_ref, species_ref, send1_ref, acc1_ref)
    pl.semaphore_wait(barrier, PLANE + 1)

    def packet(send_ref, recv_ref, out, into, p, source):
        return pltpu.make_async_remote_copy(
            src_ref=send_ref.at[p],
            dst_ref=recv_ref.at[source],
            send_sem=out.at[p],
            recv_sem=into.at[source],
            device_id=owner(p),
            device_id_type=MESH,
        )

    def forward(p, source):
        return packet(send1_ref, recv1_ref, out_sem, in_sem, p, source)

    def back(p, source):
        return packet(send2_ref, recv2_ref, back_out_sem, back_in_sem, p, source)

    def send(t, carry):
        forward(lax.rem(me + t, PLANE), me).start()
        return carry

    lax.fori_loop(1, PLANE, send, 0)
    recv1_ref[me] = send1_ref[me]
    bonds(pairs_ref, pos_ref, bonds_ref, oh_ref)

    def arrive(t, p):
        @pl.when(t > 0)
        def _():
            forward(p, p).wait_recv()

    spread(me, arrive, recv1_ref, cell_ref, ext_ref, xy_ref, z_ref, acc2_ref)

    def exchange(axis, to_left, to_right, from_left, from_right):
        copies = [
            pltpu.make_async_remote_copy(
                src_ref=src,
                dst_ref=dst,
                send_sem=side_out_sem.at[2 * axis + n],
                recv_sem=side_in_sem.at[2 * axis + n],
                device_id=shifted(axis, by_how),
                device_id_type=MESH,
            )
            for n, (src, dst, by_how) in enumerate(
                ((to_left, from_right, -1), (to_right, from_left, 1))
            )
        ]
        for copy in copies:
            copy.start()
        for copy in copies:
            copy.wait()

    exchange(
        0,
        ext_ref.at[pl.ds(W, W)],
        ext_ref.at[pl.ds(CX, W)],
        ext_ref.at[pl.ds(0, W)],
        ext_ref.at[pl.ds(W + CX, W)],
    )
    filter_x(ext_ref, ey_ref, yside_ref.at[0], yside_ref.at[1])
    exchange(1, *(yside_ref.at[n] for n in range(4)))
    filter_y(yside_ref.at[2], yside_ref.at[3], ey_ref, ay_ref, zside_ref.at[0], zside_ref.at[1])
    exchange(2, *(zside_ref.at[n] for n in range(4)))
    slopes(
        zside_ref.at[2],
        zside_ref.at[3],
        op_ref,
        hop_ref,
        ay_ref,
        smooth_ref,
        table_ref,
        p_ref,
        pz_ref,
    )

    def leave(p):
        @pl.when(p != me)
        def _():
            back(p, me).start()

    lookup(me, leave, table_ref, cell_ref, send2_ref)
    recv2_ref[me] = send2_ref[me]

    def finish(t, carry):
        p = lax.rem(me + t, PLANE)
        forward(p, me).wait_send()
        back(p, me).wait_send()
        source = lax.rem(me - t + PLANE, PLANE)
        back(source, source).wait_recv()
        return carry

    lax.fori_loop(1, PLANE, finish, 0)
    forces(
        recv2_ref, slot_ref, weight_ref, species_ref, vel_ref, delta_ref, hi_ref, lo_ref
    )
    constrain(pairs_ref, bonds_ref, delta_ref, pos_ref, newpos_ref, newvel_ref, oh_ref, nb_ref)


def on_device(positions, velocities, species, corner_slot, corner_weight, slot_cell, bond_pairs):
    own_op, halo_op = z_operators()
    layers = CX + 2
    scratch = [
        ((256, SLOTS), F32),
        ((PLANE, 2, SLOTS), F32),
        ((PLANE, 2, SLOTS), F32),
        ((CX * CY, SPREAD_ROWS * SLOTS), BF16),
        ((4 * CZ, SPREAD_ROWS * SLOTS), BF16),
        ((CX * CY, 4 * CZ), F32),
        ((CX + 2 * W, CY, WIDE), F32),
        ((layers, CY + 2 * W, WIDE), F32),
        ((4, layers, W, WIDE), F32),
        ((layers, YP, WIDE), F32),
        ((4, layers, 8, YP), F32),
        ((layers, YP, WIDE), F32),
        ((layers, YP, WIDE), F32),
        ((6 * WIDE, CX * CY), BF16),
        ((PLANE, 6, SLOTS), F32),
        ((PLANE, 6, SLOTS), F32),
        ((6 * PLANE, SLOTS), BF16),
        ((6 * PLANE, SLOTS), BF16),
        ((3, BEADS_DEV), F32),
        ((8, BONDS_DEV), F32),
        ((128, ENDS), BF16),
        ((128, ENDS), BF16),
    ]
    vmem = pl.BlockSpec(memory_space=pltpu.VMEM)
    outs = [((3, BEADS_DEV), F32), ((3, BEADS_DEV), F32), ((2, CX, CY, CZ), F32)]
    dma = pltpu.SemaphoreType.DMA
    moved, new_velocities, smoothed = pl.pallas_call(
        step_kernel,
        out_shape=[jax.ShapeDtypeStruct(*o) for o in outs],
        in_specs=[vmem] * 9,
        out_specs=[vmem] * 3,
        scratch_shapes=[pltpu.VMEM(*s) for s in scratch] + [dma((PLANE,))] * 4 + [dma((6,))] * 2,
        compiler_params=pltpu.CompilerParams(
            vmem_limit_bytes=60 * 1024 * 1024, collective_id=0, has_side_effects=True
        ),
        name="step",
    )(
        corner_slot,
        corner_weight,
        species[None, :],
        slot_cell,
        bond_pairs,
        positions,
        velocities,
        jnp.asarray(own_op),
        jnp.asarray(halo_op),
    )
    return (moved, new_velocities, smoothed)


def solution(mesh):
    placed = (
        P(None, OWNERS),
        P(None, OWNERS),
        P(OWNERS),
        P(None, None, OWNERS),
        P(None, OWNERS),
        P(None, OWNERS, None),
        P(None, OWNERS),
    )
    return jax.shard_map(
        on_device,
        mesh=mesh,
        in_specs=placed,
        out_specs=(P(None, OWNERS), P(None, OWNERS), P(None, "bx", "by", "bz")),
        check_vma=False,
    )
```

```python
import functools
import math

import jax
import jax.numpy as jnp
import numpy as np
from jax import lax
from jax.experimental import pallas as pl
from jax.experimental.pallas import tpu as pltpu
from jax.sharding import PartitionSpec as P

CX = 16
CY = 64
CZ = 64
BEADS_DEV = 4096
REACH = 3
SWEEPS = 4
SLOTS = 256
PLANE = 64
BONDS_DEV = 3840
OWNERS = ("bx", "by", "bz")
N_BY = 8
MESH = pl.DeviceIdType.MESH
SPREAD_ROWS = 8
GATHER_ROWS = 4
FORCE_CHUNK = 1024
YP = 72
W = REACH + 1
WIDE = 2 * CZ
HALF = BONDS_DEV
ENDS = 2 * BONDS_DEV

spread_cells = 1.0
mixing = 10.0
stiffness = 5.0
time_step = 0.1

F32 = jnp.float32
BF16 = jnp.bfloat16
F8 = jnp.float8_e4m3fn
NT = (((1,), (1,)), ((), ()))
NN = (((1,), (0,)), ((), ()))


def gauss_taps():
    raw_list = [
        math.exp(-0.5 * (offset - REACH) ** 2 / spread_cells**2) for offset in range(2 * REACH + 1)
    ]
    tap_total = sum(raw_list)
    return [entry / tap_total for entry in raw_list]


def mm(a, b, dims=NN):
    return lax.dot_general(a, b, dims, preferred_element_type=F32)


def two(x):
    hi = x.astype(BF16)
    return hi, (x - hi.astype(F32)).astype(BF16)


def three(x):
    hi = x.astype(BF16)
    rest = x - hi.astype(F32)
    mid = rest.astype(BF16)
    return hi, mid, (rest - mid.astype(F32)).astype(BF16)


PIECES = 3
SHRINK = 2.0**-4


def scales(biggest):
    power = 7.0 - jnp.ceil(jnp.log2(jnp.maximum(biggest, 1e-30)))
    return jnp.exp2(power), jnp.exp2(-power)


def pieces(x, scale):
    rest = x * scale
    out = []
    for n in range(PIECES):
        out.append(rest.astype(F8))
        rest = (rest - out[-1].astype(F32)) * (1.0 / SHRINK)
    return out


def mm_pieces(table_ref, columns):
    depth = table_ref.shape[1] // PIECES
    total = mm(table_ref[:, :depth], columns[0])
    for n in range(1, PIECES):
        total = total + mm(table_ref[:, n * depth : (n + 1) * depth], columns[n])
    return total


def onehot8(index, rows):
    mask = lax.broadcasted_iota(jnp.int32, (rows, index.shape[1]), 0).astype(
        jnp.int8
    ) == index.astype(jnp.int8)
    return [
        jnp.where(mask, jnp.asarray(SHRINK**n, F8), jnp.zeros((), F8)) for n in range(PIECES)
    ]


def onehot8_xy(x, y):
    oys = onehot8(y, CY)
    xb = jnp.broadcast_to(x.astype(F32).astype(BF16), oys[0].shape)
    zero = jnp.zeros((), F8)
    masks = [xb == jnp.asarray(i, BF16) for i in range(CX)]
    return [jnp.concatenate([jnp.where(m, oy, zero) for m in masks], axis=0) for oy in oys]


def rows_iota(rows, n, dtype=BF16):
    return lax.broadcasted_iota(jnp.int32, (rows, n), 0).astype(F32).astype(dtype)


def onehot(index, rows):
    return jnp.where(
        rows_iota(rows, index.shape[1]) == index.astype(F32).astype(BF16),
        jnp.ones((), BF16),
        jnp.zeros((), BF16),
    )


def weighted(index, rows, value):
    return jnp.where(
        rows_iota(rows, index.shape[1]) == index.astype(F32).astype(BF16),
        value,
        jnp.zeros((), BF16),
    )


def pick(index, rows, values):
    n = index.shape[1]
    mask = lax.broadcasted_iota(jnp.int32, (rows, n), 0) == index
    return [
        jnp.sum(jnp.where(mask, values[g * rows : (g + 1) * rows], 0.0), axis=0, keepdims=True)
        for g in range(values.shape[0] // rows)
    ]


def onehot_xy(x, y, planes):
    oy = onehot(y, CY)
    xb = x.astype(F32).astype(BF16)
    zero = jnp.zeros((), BF16)
    return jnp.concatenate([jnp.where(xb == jnp.asarray(i, BF16), oy, zero) for i in planes], axis=0)


def z_operators():
    taps = gauss_taps()
    w = REACH + 1
    smooth = np.zeros((CZ + 2 * w, CZ))
    slope = np.zeros((CZ + 2 * w, CZ))
    for z in range(CZ):
        for j in range(2 * REACH + 1):
            smooth[z + w + j - REACH, z] += taps[j]
            slope[z + w + 1 + j - REACH, z] += 0.5 * taps[j]
            slope[z + w - 1 + j - REACH, z] -= 0.5 * taps[j]
    mix = np.array([[stiffness, mixing + stiffness], [mixing + stiffness, stiffness]])
    full = np.concatenate(
        [np.kron(np.eye(2), smooth), np.kron(mix.T, smooth), np.kron(mix.T, slope)], axis=1
    ).reshape(2, CZ + 2 * w, 6 * CZ)
    own = full[:, w : w + CZ].reshape(2 * CZ, 6 * CZ)
    halo = np.concatenate(
        [full[:, :w].reshape(2 * w, 6 * CZ), full[:, w + CZ :].reshape(2 * w, 6 * CZ)]
    )
    return own.astype(np.float32), halo.astype(np.float32)


def mm3(a, b_hi, b_lo):
    a_hi, a_lo = two(a)
    return mm(a_hi, b_hi) + (mm(a_hi, b_lo) + mm(a_lo, b_hi))


def to_rows(x):
    return jnp.concatenate([x[:, i : i + 128] for i in range(0, x.shape[1], 128)], axis=0)


def to_line(x):
    return jnp.concatenate([x[i : i + 1] for i in range(x.shape[0])], axis=1)


def pack(slot_ref, weight_ref, species_ref, send_ref, acc_ref):
    acc_ref[...] = jnp.zeros_like(acc_ref)

    def body(c, carry):
        brick = slot_ref[0, pl.ds(c, 1), :]
        slot = slot_ref[1, pl.ds(c, 1), :]
        kd = brick + PLANE * species_ref[...]
        hi, lo = two(weight_ref[pl.ds(c, 1), :])
        left = jnp.concatenate([weighted(kd, 2 * PLANE, hi), weighted(kd, 2 * PLANE, lo)], axis=0)
        acc_ref[...] += mm(left, onehot(slot, SLOTS), NT)
        return carry

    lax.fori_loop(0, 8, body, 0)
    total = acc_ref[: 2 * PLANE] + acc_ref[2 * PLANE :]
    send_ref[:, 0, :] = total[:PLANE]
    send_ref[:, 1, :] = total[PLANE:]


EDGE = tuple(range(W)) + tuple(range(CX - W, CX))
INNER = tuple(range(W, CX - W))


def spread(me, arrive, edge_done, recv_ref, cell_ref, ext_ref, xy_ref, z_ref, acc_ref):
    span = SPREAD_ROWS * SLOTS

    def source(t):
        return lax.rem(me - t + PLANE, PLANE)

    def put_z(step):
        for i in range(SPREAD_ROWS):
            t = step * SPREAD_ROWS + i
            arrive(t, source(t))
        for i in range(SPREAD_ROWS):
            p = source(step * SPREAD_ROWS + i)
            z = cell_ref[2, pl.ds(p, 1), :]
            cols = slice(i * SLOTS, (i + 1) * SLOTS)
            for k in range(2):
                hi, lo = two(recv_ref[p, k : k + 1, :])
                z_ref[step, k * CZ : (k + 1) * CZ, cols] = weighted(z, CZ, hi)
                z_ref[step, (2 + k) * CZ : (3 + k) * CZ, cols] = weighted(z, CZ, lo)

    def part(planes, with_z):
        acc_ref[...] = jnp.zeros_like(acc_ref)

        def body(step, carry):
            if with_z:
                put_z(step)
            for i in range(SPREAD_ROWS):
                p = source(step * SPREAD_ROWS + i)
                x, y = (cell_ref[a, pl.ds(p, 1), :] for a in range(2))
                xy_ref[:, i * SLOTS : (i + 1) * SLOTS] = onehot_xy(x, y, planes)
            acc_ref[...] += mm(xy_ref[...], z_ref[step], NT)
            return carry

        lax.fori_loop(0, PLANE // SPREAD_ROWS, body, 0)
        total = (acc_ref[:, :WIDE] + acc_ref[:, WIDE:]) * (CX * CY * CZ / BEADS_DEV)
        return total.reshape(len(planes), CY, WIDE)

    edge = part(EDGE, True)
    ext_ref[W : 2 * W] = edge[:W]
    ext_ref[CX : CX + W] = edge[W:]
    edge_done()
    ext_ref[2 * W : CX] = part(INNER, False)


def filter_x(ext_ref, ey_ref, head_ref, tail_ref):
    taps = gauss_taps()

    def body(i, carry):
        total = taps[0] * ext_ref[i]
        for j in range(1, 2 * REACH + 1):
            total = total + taps[j] * ext_ref[i + j]
        ey_ref[i, W : W + CY] = total
        head_ref[i] = total[:W]
        tail_ref[i] = total[CY - W :]
        return carry

    lax.fori_loop(0, CX + 2, body, 0, unroll=3)


def filter_y(left_ref, right_ref, ey_ref, ay_ref, head_ref, tail_ref):
    taps = gauss_taps()
    span = CY + 2
    row = lax.broadcasted_iota(jnp.int32, (16, WIDE), 0)
    lane = lax.broadcasted_iota(jnp.int32, (16, WIDE), 1)
    wanted = ((row % 8) // W) * CZ + (row // 8) * (CZ - W) + row % W
    select = jnp.where(lane == wanted, 1.0, 0.0).astype(BF16)
    ey_ref[:, :W] = left_ref[...]
    ey_ref[:, W + CY :] = right_ref[...]

    def body(i, carry):
        total = taps[0] * ey_ref[i, :span]
        for j in range(1, 2 * REACH + 1):
            total = total + taps[j] * ey_ref[i, j : j + span]
        full = jnp.concatenate([total, jnp.zeros((YP - span, WIDE), F32)], axis=0)
        ay_ref[i] = full
        hi, mid, lo = three(full)
        edge = mm(select, hi, NT) + mm(select, mid, NT) + mm(select, lo, NT)
        head_ref[i] = edge[:8]
        tail_ref[i] = edge[8:]
        return carry

    lax.fori_loop(0, CX + 2, body, 0, unroll=3)


def slopes(
    left_ref, right_ref, op_ref, hop_ref, ay_ref, smooth_ref, table_ref, p_ref, pz_ref, slope_ref
):
    op_hi, op_lo = two(op_ref[...])
    hop_hi, hop_lo = two(hop_ref[...])

    def filter_z(i, carry):
        halo = jnp.concatenate([left_ref[i], right_ref[i]], axis=0).T
        both = mm3(ay_ref[i], op_hi, op_lo) + mm3(halo, hop_hi, hop_lo)
        smooth_ref[i] = both[1 : CY + 1, :WIDE]
        p_ref[i] = both[:, WIDE : 2 * WIDE]
        pz_ref[i] = both[:, 2 * WIDE :]
        return carry

    lax.fori_loop(0, CX + 2, filter_z, 0, unroll=3)

    biggest = jnp.zeros((CY, WIDE), F32)
    for q in range(1, CX + 1):
        sx = (p_ref[q + 1, 1 : CY + 1] - p_ref[q - 1, 1 : CY + 1]) * 0.5
        sy = (p_ref[q, 2 : CY + 2] - p_ref[q, :CY]) * 0.5
        sz = pz_ref[q, 1 : CY + 1]
        for a, slope in enumerate((sx, sy, sz)):
            slope_ref[a, (q - 1) * CY : q * CY] = slope
            biggest = jnp.maximum(biggest, jnp.abs(slope))
    scale, inverse = scales(jnp.max(biggest))
    for i in range(0, CX * CY, 128):
        for a in range(3):
            for n, piece in enumerate(pieces(slope_ref[a, i : i + 128].T, scale)):
                table_ref[a * WIDE : (a + 1) * WIDE, n * CX * CY + i : n * CX * CY + i + 128] = piece
    return inverse


def lookup(me, leave, table_ref, inverse, cell_ref, send_ref, a, b):
    def owners(t):
        return [lax.rem(me + 1 + t * GATHER_ROWS + i + PLANE, PLANE) for i in range(GATHER_ROWS)]

    def place(t, axis):
        return jnp.concatenate([cell_ref[axis, pl.ds(p, 1), :] for p in owners(t)], axis=1)

    def build(t, refs):
        for n, columns in enumerate(onehot8_xy(place(t, 0), place(t, 1))):
            refs[0][n] = columns

    def multiply(refs):
        refs[1][...] = mm_pieces(table_ref, refs[0][...])

    def choose(t, refs):
        found = pick(place(t, 2), CZ, refs[1][...])
        for i, p in enumerate(owners(t)):
            cols = slice(i * SLOTS, (i + 1) * SLOTS)
            send_ref[p] = jnp.concatenate([found[g][:, cols] for g in range(6)], axis=0) * inverse

    b[1][...] = jnp.zeros_like(b[1])
    build(0, a)
    steps = PLANE // GATHER_ROWS

    def body(s, carry):
        t = 2 * s
        multiply(a)
        build(t + 1, b)
        choose(t - 1, b)
        multiply(b)
        build(t + 2, a)
        choose(t, a)

        @pl.when(s > 0)
        def _():
            for p in owners(t - 1):
                leave(p)

        for p in owners(t):
            leave(p)
        return carry

    lax.fori_loop(0, steps // 2, body, 0)
    choose(steps - 1, b)
    for p in owners(steps - 1)[:-1]:
        leave(p)


def forces(recv_ref, slot_ref, weight_ref, species_ref, vel_ref, delta_ref, table_ref):
    for g in range(6):
        for n, part in enumerate(two(recv_ref[:, g, :])):
            table_ref[(6 * n + g) * PLANE : (6 * n + g + 1) * PLANE] = part
    wide = 2 * PLANE
    half = 6 * PLANE

    def body(step, carry):
        cols = pl.ds(pl.multiple_of(step * FORCE_CHUNK, FORCE_CHUNK), FORCE_CHUNK)
        species = species_ref[:, cols]
        force = [jnp.zeros((1, FORCE_CHUNK), F32)] * 3
        for c in range(8):
            both = mm(table_ref[...], onehot(slot_ref[1, c : c + 1, cols], SLOTS))
            brick = slot_ref[0, c : c + 1, cols] + PLANE * species
            found = pick(brick, wide, both[:half] + both[half:])
            weight = weight_ref[c : c + 1, cols]
            force = [force[a] - weight * found[a] for a in range(3)]
        for a in range(3):
            half_step = vel_ref[a : a + 1, cols] + 0.5 * time_step * force[a]
            delta_ref[a : a + 1, cols] = time_step * half_step
        return carry

    lax.fori_loop(0, BEADS_DEV // FORCE_CHUNK, body, 0)


def bonds(pairs_ref, positions_ref, out_ref, oh_ref):
    pairs = jnp.concatenate([pairs_ref[0:1], pairs_ref[1:2]], axis=1)
    hi_index = pairs >> 7
    oh_ref[...] = onehot(pairs & 127, 128)
    number = lax.broadcasted_iota(jnp.int32, (1, HALF), 1)
    number = jnp.concatenate([number, number], axis=1)
    sign = jnp.where(lax.broadcasted_iota(jnp.int32, (1, ENDS), 1) < HALF, 1.0, -1.0)
    left = jnp.concatenate(
        [
            weighted(hi_index, 32, v.astype(F32).astype(BF16))
            for v in (number >> 6, number & 63, sign)
        ],
        axis=0,
    )
    sums = mm(left, oh_ref[...], NT).astype(BF16)
    high, low, signs = pick(hi_index, 32, mm(sums, oh_ref[...]))
    other = 64.0 * high + low - number.astype(F32)
    other_sign = signs - sign
    parts = [three(to_rows(positions_ref[a : a + 1])) for a in range(3)]
    table = [jnp.concatenate([parts[a][q] for a in range(3)], axis=0) for q in range(3)]
    oh = oh_ref[...]
    ends = pick(hi_index, 32, mm(table[0], oh) + mm(table[1], oh) + mm(table[2], oh))
    for a in range(3):
        out_ref[a : a + 1] = ends[a][:, :HALF] - ends[a][:, HALF:]
    out_ref[3:4] = other[:, :HALF]
    out_ref[4:5] = other[:, HALF:]
    out_ref[5:6] = other_sign[:, :HALF]
    out_ref[6:7] = other_sign[:, HALF:]
    out_ref[7:8] = jnp.zeros((1, HALF), F32)


def constrain(pairs_ref, bonds_ref, delta_ref, pos_ref, newpos_ref, newvel_ref, oh_ref, nb_ref):
    pairs = jnp.concatenate([pairs_ref[0:1], pairs_ref[1:2]], axis=1)
    hi_index = pairs >> 7
    oh_ref[...] = onehot(pairs & 127, 128)
    r = [bonds_ref[a : a + 1] for a in range(3)]
    other = jnp.concatenate([bonds_ref[3:4], bonds_ref[4:5]], axis=1).astype(jnp.int32)
    sign = [bonds_ref[5:6], bonds_ref[6:7]]
    other_hi = other >> 7
    nb_ref[...] = onehot(other & 127, 128)
    delta = [delta_ref[a : a + 1] for a in range(3)]
    parts = [two(to_rows(d)) for d in delta]
    table = [jnp.concatenate([parts[a][q] for a in range(3)], axis=0) for q in range(2)]
    ends = pick(hi_index, 32, mm(table[0], oh_ref[...]) + mm(table[1], oh_ref[...]))
    v = [r[a] + (ends[a][:, :HALF] - ends[a][:, HALF:]) for a in range(3)]
    total = [jnp.zeros((1, HALF), F32)] * 3
    for sweep in range(SWEEPS):
        vv = v[0] * v[0] + v[1] * v[1] + v[2] * v[2]
        vr = v[0] * r[0] + v[1] * r[1] + v[2] * r[2]
        g = (vv - 1.0) / (4.0 * jnp.maximum(vr, 0.5))
        shift = [g * r[a] for a in range(3)]
        total = [total[a] + shift[a] for a in range(3)]
        if sweep + 1 == SWEEPS:
            break
        pad = jnp.zeros((2, 128), F32)
        parts = [two(jnp.concatenate([to_rows(s), pad], axis=0)) for s in shift]
        table = [jnp.concatenate([parts[a][q] for a in range(3)], axis=0) for q in range(2)]
        near = pick(other_hi, 32, mm(table[0], nb_ref[...]) + mm(table[1], nb_ref[...]))
        v = [
            v[a] - 2.0 * shift[a] - sign[0] * near[a][:, :HALF] + sign[1] * near[a][:, HALF:]
            for a in range(3)
        ]
    rows = []
    for a in range(3):
        both = jnp.concatenate([total[a], -total[a]], axis=1)
        rows += [weighted(hi_index, 32, q) for q in two(both)]
    moved = mm(jnp.concatenate(rows, axis=0), oh_ref[...], NT)
    for a in range(3):
        q = to_line(moved[64 * a : 64 * a + 32] + moved[64 * a + 32 : 64 * a + 64])
        change = delta[a] - q
        newpos_ref[a : a + 1] = pos_ref[a : a + 1] + change
        newvel_ref[a : a + 1] = change / time_step


def field_kernel(
    slot_ref,
    weight_ref,
    species_ref,
    cell_ref,
    pairs_ref,
    pos_ref,
    op_ref,
    hop_ref,
    recv2_ref,
    smooth_ref,
    bonds_ref,
    acc1_ref,
    send1_ref,
    recv1_ref,
    xy_ref,
    z_ref,
    acc2_ref,
    ext_ref,
    ey_ref,
    yside_ref,
    ay_ref,
    zside_ref,
    p_ref,
    pz_ref,
    s_ref,
    slope_ref,
    table_ref,
    send2_ref,
    cols_a_ref,
    found_a_ref,
    cols_b_ref,
    found_b_ref,
    oh_ref,
    out_sem,
    in_sem,
    back_out_sem,
    back_in_sem,
    side_out_sem,
    side_in_sem,
    own_sem,
):
    bx, by, bz = (lax.axis_index(a) for a in OWNERS)
    me = bx * N_BY + by
    counts = [lax.axis_size(a) for a in OWNERS]

    def owner(p):
        return (p // N_BY, lax.rem(p, N_BY), bz)

    def shifted(axis, by_how):
        place = [bx, by, bz]
        place[axis] = lax.rem(place[axis] + by_how + counts[axis], counts[axis])
        return tuple(place)

    barrier = pltpu.get_barrier_semaphore()

    def greet(t, carry):
        p = lax.rem(me + t, PLANE)
        pl.semaphore_signal(barrier, inc=1, device_id=owner(p), device_id_type=MESH)
        return carry

    lax.fori_loop(1, PLANE, greet, 0)
    for by_how in (-1, 1):
        pl.semaphore_signal(barrier, inc=1, device_id=shifted(2, by_how), device_id_type=MESH)

    pack(slot_ref, weight_ref, species_ref, send1_ref, acc1_ref)
    pl.semaphore_wait(barrier, PLANE + 1)

    def packet(send_ref, recv_ref, out, into, p, source):
        return pltpu.make_async_remote_copy(
            src_ref=send_ref.at[p],
            dst_ref=recv_ref.at[source],
            send_sem=out.at[p],
            recv_sem=into.at[source],
            device_id=owner(p),
            device_id_type=MESH,
        )

    def forward(p, source):
        return packet(send1_ref, recv1_ref, out_sem, in_sem, p, source)

    def back(p, source):
        return packet(send2_ref, recv2_ref, back_out_sem, back_in_sem, p, source)

    def send(t, carry):
        forward(lax.rem(me + t, PLANE), me).start()
        return carry

    lax.fori_loop(1, PLANE, send, 0)
    recv1_ref[me] = send1_ref[me]
    bonds(pairs_ref, pos_ref, bonds_ref, oh_ref)

    def arrive(t, p):
        @pl.when(t > 0)
        def _():
            forward(p, p).wait_recv()

    def sides(axis, to_left, to_right, from_left, from_right):
        return [
            pltpu.make_async_remote_copy(
                src_ref=src,
                dst_ref=dst,
                send_sem=side_out_sem.at[2 * axis + n],
                recv_sem=side_in_sem.at[2 * axis + n],
                device_id=shifted(axis, by_how),
                device_id_type=MESH,
            )
            for n, (src, dst, by_how) in enumerate(
                ((to_left, from_right, -1), (to_right, from_left, 1))
            )
        ]

    def start(copies):
        for copy in copies:
            copy.start()

    def wait(copies):
        for copy in copies:
            copy.wait()

    along_x = sides(
        0,
        ext_ref.at[pl.ds(W, W)],
        ext_ref.at[pl.ds(CX, W)],
        ext_ref.at[pl.ds(0, W)],
        ext_ref.at[pl.ds(W + CX, W)],
    )
    along_y = sides(1, *(yside_ref.at[n] for n in range(4)))
    along_z = sides(2, *(zside_ref.at[n] for n in range(4)))
    spread(
        me, arrive, lambda: start(along_x), recv1_ref, cell_ref, ext_ref, xy_ref, z_ref, acc2_ref
    )
    wait(along_x)
    filter_x(ext_ref, ey_ref, yside_ref.at[0], yside_ref.at[1])
    start(along_y)
    wait(along_y)
    filter_y(yside_ref.at[2], yside_ref.at[3], ey_ref, ay_ref, zside_ref.at[0], zside_ref.at[1])
    start(along_z)
    wait(along_z)
    inverse = slopes(
        zside_ref.at[2],
        zside_ref.at[3],
        op_ref,
        hop_ref,
        ay_ref,
        s_ref,
        table_ref,
        p_ref,
        pz_ref,
        slope_ref,
    )
    keep = pltpu.make_async_copy(s_ref.at[pl.ds(1, CX)], smooth_ref, own_sem.at[0])
    keep.start()
    lookup(
        me,
        lambda p: back(p, me).start(),
        table_ref,
        inverse,
        cell_ref,
        send2_ref,
        (cols_a_ref, found_a_ref),
        (cols_b_ref, found_b_ref),
    )
    own = pltpu.make_async_copy(send2_ref.at[me], recv2_ref.at[me], own_sem.at[1])
    own.start()

    def finish(t, carry):
        p = lax.rem(me + t, PLANE)
        forward(p, me).wait_send()
        back(p, me).wait_send()
        source = lax.rem(me - t + PLANE, PLANE)
        back(source, source).wait_recv()
        return carry

    lax.fori_loop(1, PLANE, finish, 0)
    own.wait()
    keep.wait()


def bead_kernel(
    recv_ref,
    fields_ref,
    bonds_ref,
    slot_ref,
    weight_ref,
    species_ref,
    pairs_ref,
    pos_ref,
    vel_ref,
    newpos_ref,
    newvel_ref,
    smooth_ref,
    split_ref,
    table_ref,
    delta_ref,
    oh_ref,
    nb_ref,
    sem,
):
    for k in range(2):
        split_ref[k] = fields_ref[:, :, k * CZ : (k + 1) * CZ]
    keep = pltpu.make_async_copy(split_ref, smooth_ref, sem.at[0])
    keep.start()
    forces(recv_ref, slot_ref, weight_ref, species_ref, vel_ref, delta_ref, table_ref)
    constrain(pairs_ref, bonds_ref, delta_ref, pos_ref, newpos_ref, newvel_ref, oh_ref, nb_ref)
    keep.wait()


def on_device(positions, velocities, species, corner_slot, corner_weight, slot_cell, bond_pairs):
    own_op, halo_op = z_operators()
    layers = CX + 2
    group = GATHER_ROWS * SLOTS
    scratch = [
        ((256, SLOTS), F32),
        ((PLANE, 2, SLOTS), F32),
        ((PLANE, 2, SLOTS), F32),
        ((CX * CY // 2, SPREAD_ROWS * SLOTS), BF16),
        ((PLANE // SPREAD_ROWS, 4 * CZ, SPREAD_ROWS * SLOTS), BF16),
        ((CX * CY // 2, 4 * CZ), F32),
        ((CX + 2 * W, CY, WIDE), F32),
        ((layers, CY + 2 * W, WIDE), F32),
        ((4, layers, W, WIDE), F32),
        ((layers, YP, WIDE), F32),
        ((4, layers, 8, YP), F32),
        ((layers, YP, WIDE), F32),
        ((layers, YP, WIDE), F32),
        ((layers, CY, WIDE), F32),
        ((3, CX * CY, WIDE), F32),
        ((3 * WIDE, PIECES * CX * CY), F8),
        ((PLANE, 6, SLOTS), F32),
        ((PIECES, CX * CY, group), F8),
        ((3 * WIDE, group), F32),
        ((PIECES, CX * CY, group), F8),
        ((3 * WIDE, group), F32),
        ((128, ENDS), BF16),
    ]
    vmem = pl.BlockSpec(memory_space=pltpu.VMEM)
    hbm = pl.BlockSpec(memory_space=pl.ANY)
    dma = pltpu.SemaphoreType.DMA
    limit = 60 * 1024 * 1024
    species = species[None, :]
    returned, fields, bond_data = pl.pallas_call(
        field_kernel,
        out_shape=[
            jax.ShapeDtypeStruct((PLANE, 6, SLOTS), F32),
            jax.ShapeDtypeStruct((CX, CY, WIDE), F32),
            jax.ShapeDtypeStruct((8, BONDS_DEV), F32),
        ],
        in_specs=[vmem] * 8,
        out_specs=[hbm, hbm, vmem],
        scratch_shapes=[pltpu.VMEM(*s) for s in scratch]
        + [dma((PLANE,))] * 4
        + [dma((6,))] * 2
        + [dma((2,))],
        compiler_params=pltpu.CompilerParams(
            vmem_limit_bytes=limit, collective_id=0, has_side_effects=True
        ),
        name="field",
    )(
        corner_slot,
        corner_weight,
        species,
        slot_cell,
        bond_pairs,
        positions,
        jnp.asarray(own_op),
        jnp.asarray(halo_op),
    )
    moved, new_velocities, smoothed = pl.pallas_call(
        bead_kernel,
        out_shape=[
            jax.ShapeDtypeStruct((3, BEADS_DEV), F32),
            jax.ShapeDtypeStruct((3, BEADS_DEV), F32),
            jax.ShapeDtypeStruct((2, CX, CY, CZ), F32),
        ],
        in_specs=[vmem] * 9,
        out_specs=[vmem, vmem, hbm],
        scratch_shapes=[
            pltpu.VMEM((2, CX, CY, CZ), F32),
            pltpu.VMEM((12 * PLANE, SLOTS), BF16),
            pltpu.VMEM((3, BEADS_DEV), F32),
            pltpu.VMEM((128, ENDS), BF16),
            pltpu.VMEM((128, ENDS), BF16),
            dma((1,)),
        ],
        compiler_params=pltpu.CompilerParams(vmem_limit_bytes=limit),
        name="bead",
    )(
        returned,
        fields,
        bond_data,
        corner_slot,
        corner_weight,
        species,
        bond_pairs,
        positions,
        velocities,
    )
    return (moved, new_velocities, smoothed)


def solution(mesh):
    placed = (
        P(None, OWNERS),
        P(None, OWNERS),
        P(OWNERS),
        P(None, None, OWNERS),
        P(None, OWNERS),
        P(None, OWNERS, None),
        P(None, OWNERS),
    )
    return jax.shard_map(
        on_device,
        mesh=mesh,
        in_specs=placed,
        out_specs=(P(None, OWNERS), P(None, OWNERS), P(None, "bx", "by", "bz")),
        check_vma=False,
    )
```

```python
import functools
import math

import jax
import jax.numpy as jnp
import numpy as np
from jax import lax
from jax.experimental import pallas as pl
from jax.experimental.pallas import tpu as pltpu
from jax.sharding import PartitionSpec as P

CX = 16
CY = 64
CZ = 64
BEADS_DEV = 4096
REACH = 3
SWEEPS = 4
SLOTS = 256
PLANE = 64
BONDS_DEV = 3840
OWNERS = ("bx", "by", "bz")
N_BY = 8
MESH = pl.DeviceIdType.MESH
SPREAD_ROWS = 8
GATHER_ROWS = 4
BACK = 8
FORCE_CHUNK = 1024
YP = 72
W = REACH + 1
WIDE = 2 * CZ
HALF = BONDS_DEV
ENDS = 2 * BONDS_DEV

spread_cells = 1.0
mixing = 10.0
stiffness = 5.0
time_step = 0.1

F32 = jnp.float32
BF16 = jnp.bfloat16
F8 = jnp.float8_e4m3fn
NT = (((1,), (1,)), ((), ()))
NN = (((1,), (0,)), ((), ()))


def gauss_taps():
    raw_list = [
        math.exp(-0.5 * (offset - REACH) ** 2 / spread_cells**2) for offset in range(2 * REACH + 1)
    ]
    tap_total = sum(raw_list)
    return [entry / tap_total for entry in raw_list]


def mm(a, b, dims=NN):
    return lax.dot_general(a, b, dims, preferred_element_type=F32)


def two(x):
    hi = x.astype(BF16)
    return hi, (x - hi.astype(F32)).astype(BF16)


def three(x):
    hi = x.astype(BF16)
    rest = x - hi.astype(F32)
    mid = rest.astype(BF16)
    return hi, mid, (rest - mid.astype(F32)).astype(BF16)


PIECES = 3
SHRINK = 2.0**-4
WEIGHT_SCALE = 128.0


def scales(biggest):
    power = 7.0 - jnp.ceil(jnp.log2(jnp.maximum(biggest, 1e-30)))
    return jnp.exp2(power), jnp.exp2(-power)


def pieces(x, scale):
    rest = x * scale
    out = []
    for n in range(PIECES):
        out.append(rest.astype(F8))
        rest = (rest - out[-1].astype(F32)) * (1.0 / SHRINK)
    return out


def mm_pieces(table_ref, columns):
    depth = table_ref.shape[1] // PIECES
    total = mm(table_ref[:, :depth], columns[0])
    for n in range(1, PIECES):
        total = total + mm(table_ref[:, n * depth : (n + 1) * depth], columns[n])
    return total


def same8(index, rows):
    row = lax.broadcasted_iota(jnp.int32, (rows, index.shape[1]), 0)
    return row.astype(jnp.int8) == index.astype(jnp.int8)


def onehot8(index, rows):
    mask = same8(index, rows)
    return [
        jnp.where(mask, jnp.asarray(SHRINK**n, F8), jnp.zeros((), F8)) for n in range(PIECES)
    ]


def onehot8_xy(x, y):
    oys = onehot8(y, CY)
    xb = jnp.broadcast_to(x.astype(F32).astype(BF16), oys[0].shape)
    zero = jnp.zeros((), F8)
    masks = [xb == jnp.asarray(i, BF16) for i in range(CX)]
    return [jnp.concatenate([jnp.where(m, oy, zero) for m in masks], axis=0) for oy in oys]


def rows_iota(rows, n, dtype=BF16):
    return lax.broadcasted_iota(jnp.int32, (rows, n), 0).astype(F32).astype(dtype)


def onehot(index, rows):
    return jnp.where(
        rows_iota(rows, index.shape[1]) == index.astype(F32).astype(BF16),
        jnp.ones((), BF16),
        jnp.zeros((), BF16),
    )


def weighted(index, rows, value):
    return jnp.where(
        rows_iota(rows, index.shape[1]) == index.astype(F32).astype(BF16),
        value,
        jnp.zeros((), BF16),
    )


def pick(index, rows, values):
    n = index.shape[1]
    mask = lax.broadcasted_iota(jnp.int32, (rows, n), 0) == index
    return [
        jnp.sum(jnp.where(mask, values[g * rows : (g + 1) * rows], 0.0), axis=0, keepdims=True)
        for g in range(values.shape[0] // rows)
    ]


def onehot_xy(x, y, planes):
    oy = onehot(y, CY)
    xb = x.astype(F32).astype(BF16)
    zero = jnp.zeros((), BF16)
    return jnp.concatenate([jnp.where(xb == jnp.asarray(i, BF16), oy, zero) for i in planes], axis=0)


def z_operators():
    taps = gauss_taps()
    w = REACH + 1
    smooth = np.zeros((CZ + 2 * w, CZ))
    slope = np.zeros((CZ + 2 * w, CZ))
    for z in range(CZ):
        for j in range(2 * REACH + 1):
            smooth[z + w + j - REACH, z] += taps[j]
            slope[z + w + 1 + j - REACH, z] += 0.5 * taps[j]
            slope[z + w - 1 + j - REACH, z] -= 0.5 * taps[j]
    mix = np.array([[stiffness, mixing + stiffness], [mixing + stiffness, stiffness]])
    full = np.concatenate(
        [np.kron(np.eye(2), smooth), np.kron(mix.T, smooth), np.kron(mix.T, slope)], axis=1
    ).reshape(2, CZ + 2 * w, 6 * CZ)
    own = full[:, w : w + CZ].reshape(2 * CZ, 6 * CZ)
    halo = np.concatenate(
        [full[:, :w].reshape(2 * w, 6 * CZ), full[:, w + CZ :].reshape(2 * w, 6 * CZ)]
    )
    return own.astype(np.float32), halo.astype(np.float32)


def mm3(a, b_hi, b_lo):
    a_hi, a_lo = two(a)
    return mm(a_hi, b_hi) + (mm(a_hi, b_lo) + mm(a_lo, b_hi))


def to_rows(x):
    return jnp.concatenate([x[:, i : i + 128] for i in range(0, x.shape[1], 128)], axis=0)


def to_line(x):
    return jnp.concatenate([x[i : i + 1] for i in range(x.shape[0])], axis=1)


def pack(slot_ref, weight_ref, species_ref, send_ref, acc_ref):
    acc_ref[...] = jnp.zeros_like(acc_ref)

    def body(c, carry):
        brick = slot_ref[0, pl.ds(c, 1), :]
        slot = slot_ref[1, pl.ds(c, 1), :]
        mask = same8(brick + PLANE * species_ref[...], 2 * PLANE)
        left = [
            jnp.where(mask, jnp.broadcast_to(piece, mask.shape), jnp.zeros((), F8))
            for piece in pieces(weight_ref[pl.ds(c, 1), :], WEIGHT_SCALE)
        ]
        right = jnp.where(same8(slot, SLOTS), jnp.ones((), F8), jnp.zeros((), F8))
        acc_ref[...] += mm(jnp.concatenate(left, axis=0), right, NT)
        return carry

    lax.fori_loop(0, 8, body, 0)
    rows = 2 * PLANE
    total = acc_ref[(PIECES - 1) * rows :]
    for n in range(PIECES - 2, -1, -1):
        total = acc_ref[n * rows : (n + 1) * rows] + SHRINK * total
    total = total * (1.0 / WEIGHT_SCALE)
    send_ref[:, 0, :] = total[:PLANE]
    send_ref[:, 1, :] = total[PLANE:]


EDGE = tuple(range(W)) + tuple(range(CX - W, CX))
INNER = tuple(range(W, CX - W))


def spread(me, arrive, edge_done, recv_ref, cell_ref, ext_ref, xy_ref, z_ref, acc_ref):
    span = SPREAD_ROWS * SLOTS

    def source(t):
        return lax.rem(me - t + PLANE, PLANE)

    def put_z(step):
        for i in range(SPREAD_ROWS):
            t = step * SPREAD_ROWS + i
            arrive(t, source(t))
        for i in range(SPREAD_ROWS):
            p = source(step * SPREAD_ROWS + i)
            z = cell_ref[2, pl.ds(p, 1), :]
            cols = slice(i * SLOTS, (i + 1) * SLOTS)
            for k in range(2):
                hi, lo = two(recv_ref[p, k : k + 1, :])
                z_ref[step, k * CZ : (k + 1) * CZ, cols] = weighted(z, CZ, hi)
                z_ref[step, (2 + k) * CZ : (3 + k) * CZ, cols] = weighted(z, CZ, lo)

    def part(planes, with_z):
        acc_ref[...] = jnp.zeros_like(acc_ref)

        def body(step, carry):
            if with_z:
                put_z(step)
            for i in range(SPREAD_ROWS):
                p = source(step * SPREAD_ROWS + i)
                x, y = (cell_ref[a, pl.ds(p, 1), :] for a in range(2))
                xy_ref[:, i * SLOTS : (i + 1) * SLOTS] = onehot_xy(x, y, planes)
            acc_ref[...] += mm(xy_ref[...], z_ref[step], NT)
            return carry

        lax.fori_loop(0, PLANE // SPREAD_ROWS, body, 0)
        total = (acc_ref[:, :WIDE] + acc_ref[:, WIDE:]) * (CX * CY * CZ / BEADS_DEV)
        return total.reshape(len(planes), CY, WIDE)

    edge = part(EDGE, True)
    ext_ref[W : 2 * W] = edge[:W]
    ext_ref[CX : CX + W] = edge[W:]
    edge_done()
    ext_ref[2 * W : CX] = part(INNER, False)


def filter_x(ext_ref, ey_ref, head_ref, tail_ref):
    taps = gauss_taps()

    def body(i, carry):
        total = taps[0] * ext_ref[i]
        for j in range(1, 2 * REACH + 1):
            total = total + taps[j] * ext_ref[i + j]
        ey_ref[i, W : W + CY] = total
        head_ref[i] = total[:W]
        tail_ref[i] = total[CY - W :]
        return carry

    lax.fori_loop(0, CX + 2, body, 0, unroll=3)


def filter_rows(ey_ref, i, first, rows):
    taps = gauss_taps()
    total = taps[0] * ey_ref[i, first : first + rows]
    for j in range(1, 2 * REACH + 1):
        total = total + taps[j] * ey_ref[i, first + j : first + j + rows]
    return total


Y_LOW = 8
Y_HIGH = 56


def filter_y_inner(ey_ref, ay_ref):
    def body(i, carry):
        ay_ref[i, Y_LOW:Y_HIGH] = filter_rows(ey_ref, i, Y_LOW, Y_HIGH - Y_LOW)
        return carry

    lax.fori_loop(0, CX + 2, body, 0, unroll=3)


def filter_y_edge(left_ref, right_ref, ey_ref, ay_ref, head_ref, tail_ref):
    span = CY + 2
    row = lax.broadcasted_iota(jnp.int32, (16, WIDE), 0)
    lane = lax.broadcasted_iota(jnp.int32, (16, WIDE), 1)
    wanted = ((row % 8) // W) * CZ + (row // 8) * (CZ - W) + row % W
    select = jnp.where(lane == wanted, 1.0, 0.0).astype(BF16)
    ey_ref[:, :W] = left_ref[...]
    ey_ref[:, W + CY :] = right_ref[...]
    blank = jnp.zeros((YP - span, WIDE), F32)
    pad = jnp.zeros((WIDE - YP, WIDE), F32)

    def body(i, carry):
        low = filter_rows(ey_ref, i, 0, Y_LOW)
        high = jnp.concatenate([filter_rows(ey_ref, i, Y_HIGH, span - Y_HIGH), blank], axis=0)
        ay_ref[i, :Y_LOW] = low
        ay_ref[i, Y_HIGH:] = high
        full = jnp.concatenate([low, ay_ref[i, Y_LOW:Y_HIGH], high, pad], axis=0)
        hi, mid, lo = three(full)
        edge = mm(select, hi, NT) + mm(select, mid, NT) + mm(select, lo, NT)
        head_ref[i] = edge[:8]
        tail_ref[i] = edge[8:]
        return carry

    lax.fori_loop(0, CX + 2, body, 0, unroll=3)


def filter_z_own(op_ref, ay_ref, part_ref):
    op_hi, op_lo = two(op_ref[...])

    def body(i, carry):
        part_ref[i] = mm3(ay_ref[i], op_hi, op_lo)
        return carry

    lax.fori_loop(0, CX + 2, body, 0, unroll=3)


def slopes(
    left_ref, right_ref, hop_ref, part_ref, smooth_ref, table_ref, p_ref, pz_ref, slope_ref
):
    hop_hi, hop_lo = two(hop_ref[...])

    def filter_z(i, carry):
        halo = jnp.concatenate([left_ref[i], right_ref[i]], axis=0).T
        both = part_ref[i] + mm3(halo[:YP], hop_hi, hop_lo)
        smooth_ref[i] = both[1 : CY + 1, :WIDE]
        p_ref[i] = both[:, WIDE : 2 * WIDE]
        pz_ref[i] = both[:, 2 * WIDE :]
        return carry

    lax.fori_loop(0, CX + 2, filter_z, 0, unroll=3)
    biggest = jnp.zeros((CY, WIDE), F32)
    for q in range(1, CX + 1):
        sx = (p_ref[q + 1, 1 : CY + 1] - p_ref[q - 1, 1 : CY + 1]) * 0.5
        sy = (p_ref[q, 2 : CY + 2] - p_ref[q, :CY]) * 0.5
        sz = pz_ref[q, 1 : CY + 1]
        for a, slope in enumerate((sx, sy, sz)):
            slope_ref[a, (q - 1) * CY : q * CY] = slope
            biggest = jnp.maximum(biggest, jnp.abs(slope))
    scale, inverse = scales(jnp.max(biggest))
    for i in range(0, CX * CY, 128):
        for a in range(3):
            for n, piece in enumerate(pieces(slope_ref[a, i : i + 128].T, scale)):
                table_ref[a * WIDE : (a + 1) * WIDE, n * CX * CY + i : n * CX * CY + i + 128] = piece
    return inverse


def lookup(me, leave, table_ref, inverse, cell_ref, send_ref, a, b):
    def owners(t):
        return [lax.rem(me + 1 + t * GATHER_ROWS + i + PLANE, PLANE) for i in range(GATHER_ROWS)]

    def place(t, axis):
        return jnp.concatenate([cell_ref[axis, pl.ds(p, 1), :] for p in owners(t)], axis=1)

    def build(t, refs):
        for n, columns in enumerate(onehot8_xy(place(t, 0), place(t, 1))):
            refs[0][n] = columns

    def multiply(refs):
        refs[1][...] = mm_pieces(table_ref, refs[0][...])

    def choose(t, refs):
        found = pick(place(t, 2), CZ, refs[1][...])
        for i, p in enumerate(owners(t)):
            cols = slice(i * SLOTS, (i + 1) * SLOTS)
            blank = jnp.zeros((BACK - 6, SLOTS), F32)
            send_ref[p] = (
                jnp.concatenate([found[g][:, cols] for g in range(6)] + [blank], axis=0) * inverse
            )

    b[1][...] = jnp.zeros_like(b[1])
    build(0, a)
    steps = PLANE // GATHER_ROWS

    def body(s, carry):
        t = 2 * s
        multiply(a)
        build(t + 1, b)
        choose(t - 1, b)
        multiply(b)
        build(t + 2, a)
        choose(t, a)

        @pl.when(s > 0)
        def _():
            for p in owners(t - 1):
                leave(p)

        for p in owners(t):
            leave(p)
        return carry

    lax.fori_loop(0, steps // 2, body, 0)
    choose(steps - 1, b)
    for p in owners(steps - 1)[:-1]:
        leave(p)


def forces(recv_ref, slot_ref, weight_ref, species_ref, vel_ref, delta_ref, table_ref):
    received = recv_ref[...]
    scale, inverse = scales(jnp.max(jnp.max(jnp.abs(received), axis=0)))
    table = pltpu.einshape("dgs->gds", received)
    for g in range(6):
        for n, piece in enumerate(pieces(table[g], scale)):
            table_ref[g * PLANE : (g + 1) * PLANE, n * SLOTS : (n + 1) * SLOTS] = piece
    wide = 2 * PLANE

    def body(step, carry):
        cols = pl.ds(pl.multiple_of(step * FORCE_CHUNK, FORCE_CHUNK), FORCE_CHUNK)
        species = species_ref[:, cols]
        force = [jnp.zeros((1, FORCE_CHUNK), F32)] * 3
        for c in range(8):
            both = mm_pieces(table_ref, onehot8(slot_ref[1, c : c + 1, cols], SLOTS))
            found = pick(slot_ref[0, c : c + 1, cols] + PLANE * species, wide, both)
            weight = weight_ref[c : c + 1, cols]
            force = [force[a] - weight * found[a] for a in range(3)]
        for a in range(3):
            half = vel_ref[a : a + 1, cols] + (0.5 * time_step) * (force[a] * inverse)
            delta_ref[a : a + 1, cols] = time_step * half
        return carry

    lax.fori_loop(0, BEADS_DEV // FORCE_CHUNK, body, 0)


def bonds(pairs_ref, positions_ref, out_ref, oh_ref):
    pairs = jnp.concatenate([pairs_ref[0:1], pairs_ref[1:2]], axis=1)
    hi_index = pairs >> 7
    oh_ref[...] = onehot(pairs & 127, 128)
    number = lax.broadcasted_iota(jnp.int32, (1, HALF), 1)
    number = jnp.concatenate([number, number], axis=1)
    sign = jnp.where(lax.broadcasted_iota(jnp.int32, (1, ENDS), 1) < HALF, 1.0, -1.0)
    left = jnp.concatenate(
        [
            weighted(hi_index, 32, v.astype(F32).astype(BF16))
            for v in (number >> 6, number & 63, sign)
        ],
        axis=0,
    )
    sums = mm(left, oh_ref[...], NT).astype(BF16)
    high, low, signs = pick(hi_index, 32, mm(sums, oh_ref[...]))
    other = 64.0 * high + low - number.astype(F32)
    other_sign = signs - sign
    parts = [three(to_rows(positions_ref[a : a + 1])) for a in range(3)]
    table = [jnp.concatenate([parts[a][q] for a in range(3)], axis=0) for q in range(3)]
    oh = oh_ref[...]
    ends = pick(hi_index, 32, mm(table[0], oh) + mm(table[1], oh) + mm(table[2], oh))
    for a in range(3):
        out_ref[a : a + 1] = ends[a][:, :HALF] - ends[a][:, HALF:]
    out_ref[3:4] = other[:, :HALF]
    out_ref[4:5] = other[:, HALF:]
    out_ref[5:6] = other_sign[:, :HALF]
    out_ref[6:7] = other_sign[:, HALF:]
    out_ref[7:8] = jnp.zeros((1, HALF), F32)


def constrain(pairs_ref, bonds_ref, delta_ref, pos_ref, newpos_ref, newvel_ref, oh_ref, nb_ref):
    pairs = jnp.concatenate([pairs_ref[0:1], pairs_ref[1:2]], axis=1)
    hi_index = pairs >> 7
    oh_ref[...] = onehot(pairs & 127, 128)
    r = [bonds_ref[a : a + 1] for a in range(3)]
    other = jnp.concatenate([bonds_ref[3:4], bonds_ref[4:5]], axis=1).astype(jnp.int32)
    sign = [bonds_ref[5:6], bonds_ref[6:7]]
    other_hi = other >> 7
    nb_ref[...] = onehot(other & 127, 128)
    delta = [delta_ref[a : a + 1] for a in range(3)]
    parts = [two(to_rows(d)) for d in delta]
    table = [jnp.concatenate([parts[a][q] for a in range(3)], axis=0) for q in range(2)]
    ends = pick(hi_index, 32, mm(table[0], oh_ref[...]) + mm(table[1], oh_ref[...]))
    v = [r[a] + (ends[a][:, :HALF] - ends[a][:, HALF:]) for a in range(3)]
    total = [jnp.zeros((1, HALF), F32)] * 3
    for sweep in range(SWEEPS):
        vv = v[0] * v[0] + v[1] * v[1] + v[2] * v[2]
        vr = v[0] * r[0] + v[1] * r[1] + v[2] * r[2]
        g = (vv - 1.0) / (4.0 * jnp.maximum(vr, 0.5))
        shift = [g * r[a] for a in range(3)]
        total = [total[a] + shift[a] for a in range(3)]
        if sweep + 1 == SWEEPS:
            break
        pad = jnp.zeros((2, 128), F32)
        parts = [two(jnp.concatenate([to_rows(s), pad], axis=0)) for s in shift]
        table = [jnp.concatenate([parts[a][q] for a in range(3)], axis=0) for q in range(2)]
        near = pick(other_hi, 32, mm(table[0], nb_ref[...]) + mm(table[1], nb_ref[...]))
        v = [
            v[a] - 2.0 * shift[a] - sign[0] * near[a][:, :HALF] + sign[1] * near[a][:, HALF:]
            for a in range(3)
        ]
    rows = []
    for a in range(3):
        both = jnp.concatenate([total[a], -total[a]], axis=1)
        rows += [weighted(hi_index, 32, q) for q in two(both)]
    moved = mm(jnp.concatenate(rows, axis=0), oh_ref[...], NT)
    for a in range(3):
        q = to_line(moved[64 * a : 64 * a + 32] + moved[64 * a + 32 : 64 * a + 64])
        change = delta[a] - q
        newpos_ref[a : a + 1] = pos_ref[a : a + 1] + change
        newvel_ref[a : a + 1] = change / time_step


def field_kernel(
    slot_ref,
    weight_ref,
    species_ref,
    cell_ref,
    pairs_ref,
    pos_ref,
    op_ref,
    hop_ref,
    recv2_ref,
    smooth_ref,
    bonds_ref,
    acc1_ref,
    send1_ref,
    recv1_ref,
    xy_ref,
    z_ref,
    acc2_ref,
    ext_ref,
    ey_ref,
    yside_ref,
    ay_ref,
    zside_ref,
    part_ref,
    p_ref,
    pz_ref,
    s_ref,
    slope_ref,
    table_ref,
    send2_ref,
    cols_a_ref,
    found_a_ref,
    cols_b_ref,
    found_b_ref,
    oh_ref,
    out_sem,
    in_sem,
    back_out_sem,
    back_in_sem,
    side_out_sem,
    side_in_sem,
    own_sem,
):
    bx, by, bz = (lax.axis_index(a) for a in OWNERS)
    me = bx * N_BY + by
    counts = [lax.axis_size(a) for a in OWNERS]

    def owner(p):
        return (p // N_BY, lax.rem(p, N_BY), bz)

    def shifted(axis, by_how):
        place = [bx, by, bz]
        place[axis] = lax.rem(place[axis] + by_how + counts[axis], counts[axis])
        return tuple(place)

    barrier = pltpu.get_barrier_semaphore()

    def greet(t, carry):
        p = lax.rem(me + t, PLANE)
        pl.semaphore_signal(barrier, inc=1, device_id=owner(p), device_id_type=MESH)
        return carry

    lax.fori_loop(1, PLANE, greet, 0)
    for by_how in (-1, 1):
        pl.semaphore_signal(barrier, inc=1, device_id=shifted(2, by_how), device_id_type=MESH)

    pack(slot_ref, weight_ref, species_ref, send1_ref, acc1_ref)
    pl.semaphore_wait(barrier, PLANE + 1)

    def packet(send_ref, recv_ref, out, into, p, source):
        return pltpu.make_async_remote_copy(
            src_ref=send_ref.at[p],
            dst_ref=recv_ref.at[source],
            send_sem=out.at[p],
            recv_sem=into.at[source],
            device_id=owner(p),
            device_id_type=MESH,
        )

    def forward(p, source):
        return packet(send1_ref, recv1_ref, out_sem, in_sem, p, source)

    def back(p, source):
        return packet(send2_ref, recv2_ref, back_out_sem, back_in_sem, p, source)

    def send(t, carry):
        forward(lax.rem(me + t, PLANE), me).start()
        return carry

    lax.fori_loop(1, PLANE, send, 0)
    recv1_ref[me] = send1_ref[me]
    bonds(pairs_ref, pos_ref, bonds_ref, oh_ref)

    def arrive(t, p):
        @pl.when(t > 0)
        def _():
            forward(p, p).wait_recv()

    def sides(axis, to_left, to_right, from_left, from_right):
        return [
            pltpu.make_async_remote_copy(
                src_ref=src,
                dst_ref=dst,
                send_sem=side_out_sem.at[2 * axis + n],
                recv_sem=side_in_sem.at[2 * axis + n],
                device_id=shifted(axis, by_how),
                device_id_type=MESH,
            )
            for n, (src, dst, by_how) in enumerate(
                ((to_left, from_right, -1), (to_right, from_left, 1))
            )
        ]

    def start(copies):
        for copy in copies:
            copy.start()

    def wait(copies):
        for copy in copies:
            copy.wait()

    along_x = sides(
        0,
        ext_ref.at[pl.ds(W, W)],
        ext_ref.at[pl.ds(CX, W)],
        ext_ref.at[pl.ds(0, W)],
        ext_ref.at[pl.ds(W + CX, W)],
    )
    along_y = sides(1, *(yside_ref.at[n] for n in range(4)))
    along_z = sides(2, *(zside_ref.at[n] for n in range(4)))
    spread(
        me, arrive, lambda: start(along_x), recv1_ref, cell_ref, ext_ref, xy_ref, z_ref, acc2_ref
    )
    wait(along_x)
    filter_x(ext_ref, ey_ref, yside_ref.at[0], yside_ref.at[1])
    start(along_y)
    filter_y_inner(ey_ref, ay_ref)
    wait(along_y)
    filter_y_edge(
        yside_ref.at[2], yside_ref.at[3], ey_ref, ay_ref, zside_ref.at[0], zside_ref.at[1]
    )
    start(along_z)
    filter_z_own(op_ref, ay_ref, part_ref)
    wait(along_z)
    inverse = slopes(
        zside_ref.at[2],
        zside_ref.at[3],
        hop_ref,
        part_ref,
        s_ref,
        table_ref,
        p_ref,
        pz_ref,
        slope_ref,
    )
    keep = pltpu.make_async_copy(s_ref.at[pl.ds(1, CX)], smooth_ref, own_sem.at[0])
    keep.start()
    lookup(
        me,
        lambda p: back(p, me).start(),
        table_ref,
        inverse,
        cell_ref,
        send2_ref,
        (cols_a_ref, found_a_ref),
        (cols_b_ref, found_b_ref),
    )
    own = pltpu.make_async_copy(send2_ref.at[me], recv2_ref.at[me], own_sem.at[1])
    own.start()

    def finish(t, carry):
        p = lax.rem(me + t, PLANE)
        forward(p, me).wait_send()
        back(p, me).wait_send()
        source = lax.rem(me - t + PLANE, PLANE)
        back(source, source).wait_recv()
        return carry

    lax.fori_loop(1, PLANE, finish, 0)
    own.wait()
    keep.wait()


def bead_kernel(
    recv_ref,
    fields_ref,
    bonds_ref,
    slot_ref,
    weight_ref,
    species_ref,
    pairs_ref,
    pos_ref,
    vel_ref,
    newpos_ref,
    newvel_ref,
    smooth_ref,
    split_ref,
    table_ref,
    delta_ref,
    oh_ref,
    nb_ref,
    sem,
):
    for k in range(2):
        split_ref[k] = fields_ref[:, :, k * CZ : (k + 1) * CZ]
    keep = pltpu.make_async_copy(split_ref, smooth_ref, sem.at[0])
    keep.start()
    forces(recv_ref, slot_ref, weight_ref, species_ref, vel_ref, delta_ref, table_ref)
    constrain(pairs_ref, bonds_ref, delta_ref, pos_ref, newpos_ref, newvel_ref, oh_ref, nb_ref)
    keep.wait()


def on_device(positions, velocities, species, corner_slot, corner_weight, slot_cell, bond_pairs):
    own_op, halo_op = z_operators()
    layers = CX + 2
    group = GATHER_ROWS * SLOTS
    scratch = [
        ((PIECES * 2 * PLANE, SLOTS), F32),
        ((PLANE, 2, SLOTS), F32),
        ((PLANE, 2, SLOTS), F32),
        ((CX * CY // 2, SPREAD_ROWS * SLOTS), BF16),
        ((PLANE // SPREAD_ROWS, 4 * CZ, SPREAD_ROWS * SLOTS), BF16),
        ((CX * CY // 2, 4 * CZ), F32),
        ((CX + 2 * W, CY, WIDE), F32),
        ((layers, CY + 2 * W, WIDE), F32),
        ((4, layers, W, WIDE), F32),
        ((layers, YP, WIDE), F32),
        ((4, layers, 8, WIDE), F32),
        ((layers, YP, 3 * WIDE), F32),
        ((layers, YP, WIDE), F32),
        ((layers, YP, WIDE), F32),
        ((layers, CY, WIDE), F32),
        ((3, CX * CY, WIDE), F32),
        ((3 * WIDE, PIECES * CX * CY), F8),
        ((PLANE, BACK, SLOTS), F32),
        ((PIECES, CX * CY, group), F8),
        ((3 * WIDE, group), F32),
        ((PIECES, CX * CY, group), F8),
        ((3 * WIDE, group), F32),
        ((128, ENDS), BF16),
    ]
    vmem = pl.BlockSpec(memory_space=pltpu.VMEM)
    hbm = pl.BlockSpec(memory_space=pl.ANY)
    dma = pltpu.SemaphoreType.DMA
    limit = 40 * 1024 * 1024
    species = species[None, :]
    returned, fields, bond_data = pl.pallas_call(
        field_kernel,
        out_shape=[
            jax.ShapeDtypeStruct((PLANE, BACK, SLOTS), F32),
            jax.ShapeDtypeStruct((CX, CY, WIDE), F32),
            jax.ShapeDtypeStruct((8, BONDS_DEV), F32),
        ],
        in_specs=[vmem] * 8,
        out_specs=[hbm, hbm, vmem],
        scratch_shapes=[pltpu.VMEM(*s) for s in scratch]
        + [dma((PLANE,))] * 4
        + [dma((6,))] * 2
        + [dma((2,))],
        compiler_params=pltpu.CompilerParams(
            vmem_limit_bytes=limit, collective_id=0, has_side_effects=True
        ),
        name="field",
    )(
        corner_slot,
        corner_weight,
        species,
        slot_cell,
        bond_pairs,
        positions,
        jnp.asarray(own_op),
        jnp.asarray(halo_op),
    )
    moved, new_velocities, smoothed = pl.pallas_call(
        bead_kernel,
        out_shape=[
            jax.ShapeDtypeStruct((3, BEADS_DEV), F32),
            jax.ShapeDtypeStruct((3, BEADS_DEV), F32),
            jax.ShapeDtypeStruct((2, CX, CY, CZ), F32),
        ],
        in_specs=[vmem] * 9,
        out_specs=[vmem, vmem, hbm],
        scratch_shapes=[
            pltpu.VMEM((2, CX, CY, CZ), F32),
            pltpu.VMEM((6 * PLANE, PIECES * SLOTS), F8),
            pltpu.VMEM((3, BEADS_DEV), F32),
            pltpu.VMEM((128, ENDS), BF16),
            pltpu.VMEM((128, ENDS), BF16),
            dma((1,)),
        ],
        compiler_params=pltpu.CompilerParams(vmem_limit_bytes=limit),
        name="bead",
    )(
        returned,
        fields,
        bond_data,
        corner_slot,
        corner_weight,
        species,
        bond_pairs,
        positions,
        velocities,
    )
    return (moved, new_velocities, smoothed)


def solution(mesh):
    placed = (
        P(None, OWNERS),
        P(None, OWNERS),
        P(OWNERS),
        P(None, None, OWNERS),
        P(None, OWNERS),
        P(None, OWNERS, None),
        P(None, OWNERS),
    )
    return jax.shard_map(
        on_device,
        mesh=mesh,
        in_specs=placed,
        out_specs=(P(None, OWNERS), P(None, OWNERS), P(None, "bx", "by", "bz")),
        check_vma=False,
    )
```

```python
import functools
import math

import jax
import jax.numpy as jnp
import numpy as np
from jax import lax
from jax.experimental import pallas as pl
from jax.experimental.pallas import tpu as pltpu
from jax.sharding import PartitionSpec as P

CX = 16
CY = 64
CZ = 64
BEADS_DEV = 4096
REACH = 3
SWEEPS = 4
SLOTS = 256
PLANE = 64
BONDS_DEV = 3840
OWNERS = ("bx", "by", "bz")
N_BY = 8
MESH = pl.DeviceIdType.MESH
SPREAD_ROWS = 8
GATHER_ROWS = 4
BACK = 8
LAYERS = 6
FORCE_CHUNK = 1024
YP = 72
W = REACH + 1
WIDE = 2 * CZ
HALF = BONDS_DEV
ENDS = 2 * BONDS_DEV

spread_cells = 1.0
mixing = 10.0
stiffness = 5.0
time_step = 0.1

F32 = jnp.float32
BF16 = jnp.bfloat16
F8 = jnp.float8_e4m3fn
NT = (((1,), (1,)), ((), ()))
NN = (((1,), (0,)), ((), ()))


def gauss_taps():
    raw_list = [
        math.exp(-0.5 * (offset - REACH) ** 2 / spread_cells**2) for offset in range(2 * REACH + 1)
    ]
    tap_total = sum(raw_list)
    return [entry / tap_total for entry in raw_list]


def mm(a, b, dims=NN):
    return lax.dot_general(a, b, dims, preferred_element_type=F32)


def two(x):
    hi = x.astype(BF16)
    return hi, (x - hi.astype(F32)).astype(BF16)


def three(x):
    hi = x.astype(BF16)
    rest = x - hi.astype(F32)
    mid = rest.astype(BF16)
    return hi, mid, (rest - mid.astype(F32)).astype(BF16)


PIECES = 3
SHRINK = 2.0**-4
WEIGHT_SCALE = 128.0


def scales(biggest):
    power = 7.0 - jnp.ceil(jnp.log2(jnp.maximum(biggest, 1e-30)))
    return jnp.exp2(power), jnp.exp2(-power)


def pieces(x, scale):
    rest = x * scale
    out = []
    for n in range(PIECES):
        out.append(rest.astype(F8))
        rest = (rest - out[-1].astype(F32)) * (1.0 / SHRINK)
    return out


def mm_pieces(table_ref, columns):
    depth = table_ref.shape[1] // PIECES
    total = mm(table_ref[:, :depth], columns[0])
    for n in range(1, PIECES):
        total = total + mm(table_ref[:, n * depth : (n + 1) * depth], columns[n])
    return total


def same8(index, rows):
    row = lax.broadcasted_iota(jnp.int32, (rows, index.shape[1]), 0)
    return row.astype(jnp.int8) == index.astype(jnp.int8)


def onehot8(index, rows):
    mask = same8(index, rows)
    return [
        jnp.where(mask, jnp.asarray(SHRINK**n, F8), jnp.zeros((), F8)) for n in range(PIECES)
    ]


def onehot8_xy(x, y):
    oys = onehot8(y, CY)
    xb = jnp.broadcast_to(x.astype(F32).astype(BF16), oys[0].shape)
    zero = jnp.zeros((), F8)
    masks = [xb == jnp.asarray(i, BF16) for i in range(CX)]
    return [jnp.concatenate([jnp.where(m, oy, zero) for m in masks], axis=0) for oy in oys]


def rows_iota(rows, n, dtype=BF16):
    return lax.broadcasted_iota(jnp.int32, (rows, n), 0).astype(F32).astype(dtype)


def onehot(index, rows):
    return jnp.where(
        rows_iota(rows, index.shape[1]) == index.astype(F32).astype(BF16),
        jnp.ones((), BF16),
        jnp.zeros((), BF16),
    )


def weighted(index, rows, value):
    return jnp.where(
        rows_iota(rows, index.shape[1]) == index.astype(F32).astype(BF16),
        value,
        jnp.zeros((), BF16),
    )


def pick(index, rows, values):
    n = index.shape[1]
    mask = lax.broadcasted_iota(jnp.int32, (rows, n), 0) == index
    return [
        jnp.sum(jnp.where(mask, values[g * rows : (g + 1) * rows], 0.0), axis=0, keepdims=True)
        for g in range(values.shape[0] // rows)
    ]


def onehot_xy(x, y, planes):
    oy = onehot(y, CY)
    xb = x.astype(F32).astype(BF16)
    zero = jnp.zeros((), BF16)
    return jnp.concatenate([jnp.where(xb == jnp.asarray(i, BF16), oy, zero) for i in planes], axis=0)


def z_operators():
    taps = gauss_taps()
    w = REACH + 1
    smooth = np.zeros((CZ + 2 * w, CZ))
    slope = np.zeros((CZ + 2 * w, CZ))
    for z in range(CZ):
        for j in range(2 * REACH + 1):
            smooth[z + w + j - REACH, z] += taps[j]
            slope[z + w + 1 + j - REACH, z] += 0.5 * taps[j]
            slope[z + w - 1 + j - REACH, z] -= 0.5 * taps[j]
    mix = np.array([[stiffness, mixing + stiffness], [mixing + stiffness, stiffness]])
    full = np.concatenate(
        [np.kron(np.eye(2), smooth), np.kron(mix.T, smooth), np.kron(mix.T, slope)], axis=1
    ).reshape(2, CZ + 2 * w, 6 * CZ)
    own = full[:, w : w + CZ].reshape(2 * CZ, 6 * CZ)
    halo = np.concatenate(
        [full[:, :w].reshape(2 * w, 6 * CZ), full[:, w + CZ :].reshape(2 * w, 6 * CZ)]
    )
    return own.astype(np.float32), halo.astype(np.float32)


def mm3(a, b_hi, b_lo):
    a_hi, a_lo = two(a)
    return mm(a_hi, b_hi) + (mm(a_hi, b_lo) + mm(a_lo, b_hi))


def to_rows(x):
    return jnp.concatenate([x[:, i : i + 128] for i in range(0, x.shape[1], 128)], axis=0)


def to_line(x):
    return jnp.concatenate([x[i : i + 1] for i in range(x.shape[0])], axis=1)


def pack(slot_ref, weight_ref, species_ref, send_ref, acc_ref):
    acc_ref[...] = jnp.zeros_like(acc_ref)

    def body(c, carry):
        brick = slot_ref[0, pl.ds(c, 1), :]
        slot = slot_ref[1, pl.ds(c, 1), :]
        mask = same8(brick + PLANE * species_ref[...], 2 * PLANE)
        left = [
            jnp.where(mask, jnp.broadcast_to(piece, mask.shape), jnp.zeros((), F8))
            for piece in pieces(weight_ref[pl.ds(c, 1), :], WEIGHT_SCALE)
        ]
        right = jnp.where(same8(slot, SLOTS), jnp.ones((), F8), jnp.zeros((), F8))
        acc_ref[...] += mm(jnp.concatenate(left, axis=0), right, NT)
        return carry

    lax.fori_loop(0, 8, body, 0)
    rows = 2 * PLANE
    total = acc_ref[(PIECES - 1) * rows :]
    for n in range(PIECES - 2, -1, -1):
        total = acc_ref[n * rows : (n + 1) * rows] + SHRINK * total
    total = total * (1.0 / WEIGHT_SCALE)
    send_ref[:, 0, :] = total[:PLANE]
    send_ref[:, 1, :] = total[PLANE:]


EDGE = tuple(range(W)) + tuple(range(CX - W, CX))
INNER = tuple(range(W, CX - W))


def spread(me, arrive, edge_done, recv_ref, cell_ref, ext_ref, xy_ref, z_ref, acc_ref):
    span = SPREAD_ROWS * SLOTS

    def source(t):
        return lax.rem(me - t + PLANE, PLANE)

    def put_z(step):
        for i in range(SPREAD_ROWS):
            t = step * SPREAD_ROWS + i
            arrive(t, source(t))
        for i in range(SPREAD_ROWS):
            p = source(step * SPREAD_ROWS + i)
            z = cell_ref[2, pl.ds(p, 1), :]
            cols = slice(i * SLOTS, (i + 1) * SLOTS)
            for k in range(2):
                hi, lo = two(recv_ref[p, k : k + 1, :])
                z_ref[step, k * CZ : (k + 1) * CZ, cols] = weighted(z, CZ, hi)
                z_ref[step, (2 + k) * CZ : (3 + k) * CZ, cols] = weighted(z, CZ, lo)

    def part(planes, with_z):
        acc_ref[...] = jnp.zeros_like(acc_ref)

        def body(step, carry):
            if with_z:
                put_z(step)
            for i in range(SPREAD_ROWS):
                p = source(step * SPREAD_ROWS + i)
                x, y = (cell_ref[a, pl.ds(p, 1), :] for a in range(2))
                xy_ref[:, i * SLOTS : (i + 1) * SLOTS] = onehot_xy(x, y, planes)
            acc_ref[...] += mm(xy_ref[...], z_ref[step], NT)
            return carry

        lax.fori_loop(0, PLANE // SPREAD_ROWS, body, 0)
        total = (acc_ref[:, :WIDE] + acc_ref[:, WIDE:]) * (CX * CY * CZ / BEADS_DEV)
        return total.reshape(len(planes), CY, WIDE)

    edge = part(EDGE, True)
    ext_ref[W : 2 * W] = edge[:W]
    ext_ref[CX : CX + W] = edge[W:]
    edge_done()
    ext_ref[2 * W : CX] = part(INNER, False)


def filter_x(ext_ref, ey_ref, head_ref, tail_ref):
    taps = gauss_taps()

    def body(i, carry):
        total = taps[0] * ext_ref[i]
        for j in range(1, 2 * REACH + 1):
            total = total + taps[j] * ext_ref[i + j]
        ey_ref[i, W : W + CY] = total
        head_ref[i] = total[:W]
        tail_ref[i] = total[CY - W :]
        return carry

    lax.fori_loop(0, CX + 2, body, 0, unroll=3)


def filter_rows(ey_ref, i, first, rows):
    taps = gauss_taps()
    total = taps[0] * ey_ref[i, first : first + rows]
    for j in range(1, 2 * REACH + 1):
        total = total + taps[j] * ey_ref[i, first + j : first + j + rows]
    return total


Y_LOW = 8
Y_HIGH = 56


def filter_y_inner(ey_ref, ay_ref):
    def body(i, carry):
        ay_ref[i, Y_LOW:Y_HIGH] = filter_rows(ey_ref, i, Y_LOW, Y_HIGH - Y_LOW)
        return carry

    lax.fori_loop(0, CX + 2, body, 0, unroll=3)


def filter_y_edge(left_ref, right_ref, ey_ref, ay_ref, head_ref, tail_ref):
    span = CY + 2
    ey_ref[:, :W] = left_ref[...]
    ey_ref[:, W + CY :] = right_ref[...]
    blank = jnp.zeros((YP - span, WIDE), F32)
    pad = jnp.zeros((WIDE - YP, WIDE), F32)

    def body(i, carry):
        low = filter_rows(ey_ref, i, 0, Y_LOW)
        high = jnp.concatenate([filter_rows(ey_ref, i, Y_HIGH, span - Y_HIGH), blank], axis=0)
        ay_ref[i, :Y_LOW] = low
        ay_ref[i, Y_HIGH:] = high
        full = jnp.concatenate([low, ay_ref[i, Y_LOW:Y_HIGH], high, pad], axis=0).T
        head_ref[i] = jnp.concatenate([full[:W], full[CZ : CZ + W]], axis=0)
        tail_ref[i] = jnp.concatenate([full[CZ - W : CZ], full[WIDE - W :]], axis=0)
        return carry

    lax.fori_loop(0, CX + 2, body, 0, unroll=3)


def filter_z_own(op_ref, ay_ref, part_ref):
    op_hi, op_lo = two(op_ref[...])
    twice = jnp.concatenate([op_hi, op_hi], axis=0)
    for i in range(0, CX + 2, LAYERS):
        hi, lo = two(ay_ref[i : i + LAYERS].reshape(LAYERS * YP, WIDE))
        own = mm(jnp.concatenate([hi, lo], axis=1), twice) + mm(hi, op_lo)
        part_ref[i : i + LAYERS] = own.reshape(LAYERS, YP, 3 * WIDE)


def slopes(
    left_ref, right_ref, hop_ref, part_ref, smooth_ref, table_ref, p_ref, pz_ref, slope_ref
):
    hop_hi, hop_lo = two(hop_ref[...])

    for i in range(0, CX + 2, LAYERS):
        halo = [
            jnp.concatenate([left_ref[q], right_ref[q]], axis=0).T[:YP]
            for q in range(i, i + LAYERS)
        ]
        both = mm3(jnp.concatenate(halo, axis=0), hop_hi, hop_lo)
        both = part_ref[i : i + LAYERS] + both.reshape(LAYERS, YP, 3 * WIDE)
        smooth_ref[i : i + LAYERS] = both[:, 1 : CY + 1, :WIDE]
        p_ref[i : i + LAYERS] = both[:, :, WIDE : 2 * WIDE]
        pz_ref[i : i + LAYERS] = both[:, :, 2 * WIDE :]
    biggest = jnp.zeros((CY, WIDE), F32)
    for q in range(1, CX + 1):
        sx = (p_ref[q + 1, 1 : CY + 1] - p_ref[q - 1, 1 : CY + 1]) * 0.5
        sy = (p_ref[q, 2 : CY + 2] - p_ref[q, :CY]) * 0.5
        sz = pz_ref[q, 1 : CY + 1]
        for a, slope in enumerate((sx, sy, sz)):
            slope_ref[a, (q - 1) * CY : q * CY] = slope
            biggest = jnp.maximum(biggest, jnp.abs(slope))
    scale, inverse = scales(jnp.max(biggest))
    for i in range(0, CX * CY, 128):
        for a in range(3):
            for n, piece in enumerate(pieces(slope_ref[a, i : i + 128].T, scale)):
                table_ref[a * WIDE : (a + 1) * WIDE, n * CX * CY + i : n * CX * CY + i + 128] = piece
    return inverse


def lookup(me, leave, table_ref, inverse, cell_ref, send_ref, a, b):
    def owners(t):
        return [lax.rem(me + 1 + t * GATHER_ROWS + i + PLANE, PLANE) for i in range(GATHER_ROWS)]

    def place(t, axis):
        return jnp.concatenate([cell_ref[axis, pl.ds(p, 1), :] for p in owners(t)], axis=1)

    def build(t, refs):
        for n, columns in enumerate(onehot8_xy(place(t, 0), place(t, 1))):
            refs[0][n] = columns

    def multiply(refs):
        refs[1][...] = mm_pieces(table_ref, refs[0][...])

    def choose(t, refs):
        found = pick(place(t, 2), CZ, refs[1][...])
        for i, p in enumerate(owners(t)):
            cols = slice(i * SLOTS, (i + 1) * SLOTS)
            blank = jnp.zeros((BACK - 6, SLOTS), F32)
            send_ref[p] = (
                jnp.concatenate([found[g][:, cols] for g in range(6)] + [blank], axis=0) * inverse
            )

    b[1][...] = jnp.zeros_like(b[1])
    build(0, a)
    steps = PLANE // GATHER_ROWS

    def body(s, carry):
        t = 2 * s
        multiply(a)
        build(t + 1, b)
        choose(t - 1, b)
        multiply(b)
        build(t + 2, a)
        choose(t, a)

        @pl.when(s > 0)
        def _():
            for p in owners(t - 1):
                leave(p)

        for p in owners(t):
            leave(p)
        return carry

    lax.fori_loop(0, steps // 2, body, 0)
    choose(steps - 1, b)
    for p in owners(steps - 1)[:-1]:
        leave(p)


def forces(recv_ref, slot_ref, weight_ref, species_ref, vel_ref, delta_ref, table_ref):
    received = recv_ref[...]
    scale, inverse = scales(jnp.max(jnp.max(jnp.abs(received), axis=0)))
    table = pltpu.einshape("dgs->gds", received)
    for g in range(6):
        for n, piece in enumerate(pieces(table[g], scale)):
            table_ref[g * PLANE : (g + 1) * PLANE, n * SLOTS : (n + 1) * SLOTS] = piece
    wide = 2 * PLANE

    def body(step, carry):
        cols = pl.ds(pl.multiple_of(step * FORCE_CHUNK, FORCE_CHUNK), FORCE_CHUNK)
        species = species_ref[:, cols]
        force = [jnp.zeros((1, FORCE_CHUNK), F32)] * 3
        for c in range(8):
            both = mm_pieces(table_ref, onehot8(slot_ref[1, c : c + 1, cols], SLOTS))
            found = pick(slot_ref[0, c : c + 1, cols] + PLANE * species, wide, both)
            weight = weight_ref[c : c + 1, cols]
            force = [force[a] - weight * found[a] for a in range(3)]
        for a in range(3):
            half = vel_ref[a : a + 1, cols] + (0.5 * time_step) * (force[a] * inverse)
            delta_ref[a : a + 1, cols] = time_step * half
        return carry

    lax.fori_loop(0, BEADS_DEV // FORCE_CHUNK, body, 0)


def bonds(pairs_ref, positions_ref, out_ref, oh_ref):
    pairs = jnp.concatenate([pairs_ref[0:1], pairs_ref[1:2]], axis=1)
    hi_index = pairs >> 7
    oh_ref[...] = onehot(pairs & 127, 128)
    number = lax.broadcasted_iota(jnp.int32, (1, HALF), 1)
    number = jnp.concatenate([number, number], axis=1)
    sign = jnp.where(lax.broadcasted_iota(jnp.int32, (1, ENDS), 1) < HALF, 1.0, -1.0)
    left = jnp.concatenate(
        [
            weighted(hi_index, 32, v.astype(F32).astype(BF16))
            for v in (number >> 6, number & 63, sign)
        ],
        axis=0,
    )
    sums = mm(left, oh_ref[...], NT).astype(BF16)
    high, low, signs = pick(hi_index, 32, mm(sums, oh_ref[...]))
    other = 64.0 * high + low - number.astype(F32)
    other_sign = signs - sign
    parts = [three(to_rows(positions_ref[a : a + 1])) for a in range(3)]
    table = [jnp.concatenate([parts[a][q] for a in range(3)], axis=0) for q in range(3)]
    oh = oh_ref[...]
    ends = pick(hi_index, 32, mm(table[0], oh) + mm(table[1], oh) + mm(table[2], oh))
    for a in range(3):
        out_ref[a : a + 1] = ends[a][:, :HALF] - ends[a][:, HALF:]
    out_ref[3:4] = other[:, :HALF]
    out_ref[4:5] = other[:, HALF:]
    out_ref[5:6] = other_sign[:, :HALF]
    out_ref[6:7] = other_sign[:, HALF:]
    out_ref[7:8] = jnp.zeros((1, HALF), F32)


def put_twice(ref, columns):
    ref[:128] = columns
    ref[128:] = columns


def constrain(pairs_ref, bonds_ref, delta_ref, pos_ref, newpos_ref, newvel_ref, oh_ref, nb_ref):
    pairs = jnp.concatenate([pairs_ref[0:1], pairs_ref[1:2]], axis=1)
    hi_index = pairs >> 7
    put_twice(oh_ref, onehot(pairs & 127, 128))
    r = [bonds_ref[a : a + 1] for a in range(3)]
    other = jnp.concatenate([bonds_ref[3:4], bonds_ref[4:5]], axis=1).astype(jnp.int32)
    sign = [bonds_ref[5:6], bonds_ref[6:7]]
    other_hi = other >> 7
    put_twice(nb_ref, onehot(other & 127, 128))
    delta = [delta_ref[a : a + 1] for a in range(3)]
    parts = [two(to_rows(d)) for d in delta]
    table = [jnp.concatenate([parts[a][q] for a in range(3)], axis=0) for q in range(2)]
    ends = pick(hi_index, 32, mm(jnp.concatenate(table, axis=1), oh_ref[...]))
    v = [r[a] + (ends[a][:, :HALF] - ends[a][:, HALF:]) for a in range(3)]
    total = [jnp.zeros((1, HALF), F32)] * 3
    for sweep in range(SWEEPS):
        vv = v[0] * v[0] + v[1] * v[1] + v[2] * v[2]
        vr = v[0] * r[0] + v[1] * r[1] + v[2] * r[2]
        g = (vv - 1.0) / (4.0 * jnp.maximum(vr, 0.5))
        shift = [g * r[a] for a in range(3)]
        total = [total[a] + shift[a] for a in range(3)]
        if sweep + 1 == SWEEPS:
            break
        pad = jnp.zeros((2, 128), F32)
        parts = [two(jnp.concatenate([to_rows(s), pad], axis=0)) for s in shift]
        table = [jnp.concatenate([parts[a][q] for a in range(3)], axis=0) for q in range(2)]
        near = pick(other_hi, 32, mm(jnp.concatenate(table, axis=1), nb_ref[...]))
        v = [
            v[a] - 2.0 * shift[a] - sign[0] * near[a][:, :HALF] + sign[1] * near[a][:, HALF:]
            for a in range(3)
        ]
    rows = []
    for a in range(3):
        both = jnp.concatenate([total[a], -total[a]], axis=1)
        rows += [weighted(hi_index, 32, q) for q in two(both)]
    moved = mm(jnp.concatenate(rows, axis=0), oh_ref[:128], NT)
    for a in range(3):
        q = to_line(moved[64 * a : 64 * a + 32] + moved[64 * a + 32 : 64 * a + 64])
        change = delta[a] - q
        newpos_ref[a : a + 1] = pos_ref[a : a + 1] + change
        newvel_ref[a : a + 1] = change / time_step


def field_kernel(
    slot_hbm,
    weight_hbm,
    species_hbm,
    cell_hbm,
    pairs_hbm,
    pos_hbm,
    op_hbm,
    hop_hbm,
    recv2_ref,
    smooth_ref,
    bonds_ref,
    acc1_ref,
    send1_ref,
    recv1_ref,
    xy_ref,
    z_ref,
    acc2_ref,
    ext_ref,
    ey_ref,
    yside_ref,
    ay_ref,
    zside_ref,
    part_ref,
    p_ref,
    pz_ref,
    s_ref,
    slope_ref,
    table_ref,
    send2_ref,
    cols_a_ref,
    found_a_ref,
    cols_b_ref,
    found_b_ref,
    oh_ref,
    slot_ref,
    weight_ref,
    species_ref,
    cell_ref,
    pairs_ref,
    pos_ref,
    op_ref,
    hop_ref,
    out_sem,
    in_sem,
    back_out_sem,
    back_in_sem,
    side_out_sem,
    side_in_sem,
    own_sem,
    input_sem,
):
    inputs = [
        pltpu.make_async_copy(src, dst, input_sem.at[n])
        for n, (src, dst) in enumerate(
            (
                (slot_hbm, slot_ref),
                (weight_hbm, weight_ref),
                (species_hbm, species_ref),
                (pairs_hbm, pairs_ref),
                (pos_hbm, pos_ref),
                (cell_hbm, cell_ref),
                (op_hbm, op_ref),
                (hop_hbm, hop_ref),
            )
        )
    ]
    for copy in inputs:
        copy.start()
    bx, by, bz = (lax.axis_index(a) for a in OWNERS)
    me = bx * N_BY + by
    counts = [lax.axis_size(a) for a in OWNERS]

    def owner(p):
        return (p // N_BY, lax.rem(p, N_BY), bz)

    def shifted(axis, by_how):
        place = [bx, by, bz]
        place[axis] = lax.rem(place[axis] + by_how + counts[axis], counts[axis])
        return tuple(place)

    barrier = pltpu.get_barrier_semaphore()

    def greet(t, carry):
        p = lax.rem(me + t, PLANE)
        pl.semaphore_signal(barrier, inc=1, device_id=owner(p), device_id_type=MESH)
        return carry

    lax.fori_loop(1, PLANE, greet, 0)
    for by_how in (-1, 1):
        pl.semaphore_signal(barrier, inc=1, device_id=shifted(2, by_how), device_id_type=MESH)

    for copy in inputs[:3]:
        copy.wait()
    pack(slot_ref, weight_ref, species_ref, send1_ref, acc1_ref)
    pl.semaphore_wait(barrier, PLANE + 1)

    def packet(send_ref, recv_ref, out, into, p, source):
        return pltpu.make_async_remote_copy(
            src_ref=send_ref.at[p],
            dst_ref=recv_ref.at[source],
            send_sem=out.at[p],
            recv_sem=into.at[source],
            device_id=owner(p),
            device_id_type=MESH,
        )

    def forward(p, source):
        return packet(send1_ref, recv1_ref, out_sem, in_sem, p, source)

    def back(p, source):
        return packet(send2_ref, recv2_ref, back_out_sem, back_in_sem, p, source)

    def send(t, carry):
        forward(lax.rem(me + t, PLANE), me).start()
        return carry

    lax.fori_loop(1, PLANE, send, 0)
    recv1_ref[me] = send1_ref[me]
    for copy in inputs[3:]:
        copy.wait()
    bonds(pairs_ref, pos_ref, bonds_ref, oh_ref)

    def arrive(t, p):
        @pl.when(t > 0)
        def _():
            forward(p, p).wait_recv()

    def sides(axis, to_left, to_right, from_left, from_right):
        return [
            pltpu.make_async_remote_copy(
                src_ref=src,
                dst_ref=dst,
                send_sem=side_out_sem.at[2 * axis + n],
                recv_sem=side_in_sem.at[2 * axis + n],
                device_id=shifted(axis, by_how),
                device_id_type=MESH,
            )
            for n, (src, dst, by_how) in enumerate(
                ((to_left, from_right, -1), (to_right, from_left, 1))
            )
        ]

    def start(copies):
        for copy in copies:
            copy.start()

    def wait(copies):
        for copy in copies:
            copy.wait()

    along_x = sides(
        0,
        ext_ref.at[pl.ds(W, W)],
        ext_ref.at[pl.ds(CX, W)],
        ext_ref.at[pl.ds(0, W)],
        ext_ref.at[pl.ds(W + CX, W)],
    )
    along_y = sides(1, *(yside_ref.at[n] for n in range(4)))
    along_z = sides(2, *(zside_ref.at[n] for n in range(4)))
    spread(
        me, arrive, lambda: start(along_x), recv1_ref, cell_ref, ext_ref, xy_ref, z_ref, acc2_ref
    )
    wait(along_x)
    filter_x(ext_ref, ey_ref, yside_ref.at[0], yside_ref.at[1])
    start(along_y)
    filter_y_inner(ey_ref, ay_ref)
    wait(along_y)
    filter_y_edge(
        yside_ref.at[2], yside_ref.at[3], ey_ref, ay_ref, zside_ref.at[0], zside_ref.at[1]
    )
    start(along_z)
    filter_z_own(op_ref, ay_ref, part_ref)
    wait(along_z)
    inverse = slopes(
        zside_ref.at[2],
        zside_ref.at[3],
        hop_ref,
        part_ref,
        s_ref,
        table_ref,
        p_ref,
        pz_ref,
        slope_ref,
    )
    keep = pltpu.make_async_copy(s_ref.at[pl.ds(1, CX)], smooth_ref, own_sem.at[0])
    keep.start()
    lookup(
        me,
        lambda p: back(p, me).start(),
        table_ref,
        inverse,
        cell_ref,
        send2_ref,
        (cols_a_ref, found_a_ref),
        (cols_b_ref, found_b_ref),
    )
    own = pltpu.make_async_copy(send2_ref.at[me], recv2_ref.at[me], own_sem.at[1])
    own.start()

    def finish(t, carry):
        p = lax.rem(me + t, PLANE)
        forward(p, me).wait_send()
        back(p, me).wait_send()
        source = lax.rem(me - t + PLANE, PLANE)
        back(source, source).wait_recv()
        return carry

    lax.fori_loop(1, PLANE, finish, 0)
    own.wait()
    keep.wait()


def bead_kernel(
    recv_ref,
    fields_ref,
    bonds_ref,
    slot_ref,
    weight_ref,
    species_ref,
    pairs_ref,
    pos_ref,
    vel_ref,
    newpos_ref,
    newvel_ref,
    smooth_ref,
    split_ref,
    table_ref,
    delta_ref,
    oh_ref,
    nb_ref,
    sem,
):
    for k in range(2):
        split_ref[k] = fields_ref[:, :, k * CZ : (k + 1) * CZ]
    keep = pltpu.make_async_copy(split_ref, smooth_ref, sem.at[0])
    keep.start()
    forces(recv_ref, slot_ref, weight_ref, species_ref, vel_ref, delta_ref, table_ref)
    constrain(pairs_ref, bonds_ref, delta_ref, pos_ref, newpos_ref, newvel_ref, oh_ref, nb_ref)
    keep.wait()


def on_device(positions, velocities, species, corner_slot, corner_weight, slot_cell, bond_pairs):
    own_op, halo_op = z_operators()
    species = species[None, :]
    layers = CX + 2
    group = GATHER_ROWS * SLOTS
    scratch = [
        ((PIECES * 2 * PLANE, SLOTS), F32),
        ((PLANE, 2, SLOTS), F32),
        ((PLANE, 2, SLOTS), F32),
        ((CX * CY // 2, SPREAD_ROWS * SLOTS), BF16),
        ((PLANE // SPREAD_ROWS, 4 * CZ, SPREAD_ROWS * SLOTS), BF16),
        ((CX * CY // 2, 4 * CZ), F32),
        ((CX + 2 * W, CY, WIDE), F32),
        ((layers, CY + 2 * W, WIDE), F32),
        ((4, layers, W, WIDE), F32),
        ((layers, YP, WIDE), F32),
        ((4, layers, 8, WIDE), F32),
        ((layers, YP, 3 * WIDE), F32),
        ((layers, YP, WIDE), F32),
        ((layers, YP, WIDE), F32),
        ((layers, CY, WIDE), F32),
        ((3, CX * CY, WIDE), F32),
        ((3 * WIDE, PIECES * CX * CY), F8),
        ((PLANE, BACK, SLOTS), F32),
        ((PIECES, CX * CY, group), F8),
        ((3 * WIDE, group), F32),
        ((PIECES, CX * CY, group), F8),
        ((3 * WIDE, group), F32),
        ((128, ENDS), BF16),
    ]
    scratch += [
        (a.shape, a.dtype)
        for a in (
            corner_slot,
            corner_weight,
            species,
            slot_cell,
            bond_pairs,
            positions,
            own_op,
            halo_op,
        )
    ]
    vmem = pl.BlockSpec(memory_space=pltpu.VMEM)
    hbm = pl.BlockSpec(memory_space=pl.ANY)
    dma = pltpu.SemaphoreType.DMA
    limit = 60 * 1024 * 1024
    returned, fields, bond_data = pl.pallas_call(
        field_kernel,
        out_shape=[
            jax.ShapeDtypeStruct((PLANE, BACK, SLOTS), F32),
            jax.ShapeDtypeStruct((CX, CY, WIDE), F32),
            jax.ShapeDtypeStruct((8, BONDS_DEV), F32),
        ],
        in_specs=[pl.BlockSpec(memory_space=pltpu.HBM)] * 8,
        out_specs=[hbm, hbm, vmem],
        scratch_shapes=[pltpu.VMEM(*s) for s in scratch]
        + [dma((PLANE,))] * 4
        + [dma((6,))] * 2
        + [dma((2,)), dma((8,))],
        compiler_params=pltpu.CompilerParams(
            vmem_limit_bytes=limit, collective_id=0, has_side_effects=True
        ),
        name="field",
    )(
        corner_slot,
        corner_weight,
        species,
        slot_cell,
        bond_pairs,
        positions,
        jnp.asarray(own_op),
        jnp.asarray(halo_op),
    )
    moved, new_velocities, smoothed = pl.pallas_call(
        bead_kernel,
        out_shape=[
            jax.ShapeDtypeStruct((3, BEADS_DEV), F32),
            jax.ShapeDtypeStruct((3, BEADS_DEV), F32),
            jax.ShapeDtypeStruct((2, CX, CY, CZ), F32),
        ],
        in_specs=[vmem] * 9,
        out_specs=[vmem, vmem, hbm],
        scratch_shapes=[
            pltpu.VMEM((2, CX, CY, CZ), F32),
            pltpu.VMEM((6 * PLANE, PIECES * SLOTS), F8),
            pltpu.VMEM((3, BEADS_DEV), F32),
            pltpu.VMEM((256, ENDS), BF16),
            pltpu.VMEM((256, ENDS), BF16),
            dma((1,)),
        ],
        compiler_params=pltpu.CompilerParams(vmem_limit_bytes=limit),
        name="bead",
    )(
        returned,
        fields,
        bond_data,
        corner_slot,
        corner_weight,
        species,
        bond_pairs,
        positions,
        velocities,
    )
    return (moved, new_velocities, smoothed)


def solution(mesh):
    placed = (
        P(None, OWNERS),
        P(None, OWNERS),
        P(OWNERS),
        P(None, None, OWNERS),
        P(None, OWNERS),
        P(None, OWNERS, None),
        P(None, OWNERS),
    )
    return jax.shard_map(
        on_device,
        mesh=mesh,
        in_specs=placed,
        out_specs=(P(None, OWNERS), P(None, OWNERS), P(None, "bx", "by", "bz")),
        check_vma=False,
    )
```

```python
import functools
import math

import jax
import jax.numpy as jnp
import numpy as np
from jax import lax
from jax.experimental import pallas as pl
from jax.experimental.pallas import tpu as pltpu
from jax.sharding import PartitionSpec as P

CX = 16
CY = 64
CZ = 64
BEADS_DEV = 4096
REACH = 3
SWEEPS = 4
SLOTS = 256
PLANE = 64
BONDS_DEV = 3840
OWNERS = ("bx", "by", "bz")
N_BY = 8
MESH = pl.DeviceIdType.MESH
SPREAD_ROWS = 32
GATHER_ROWS = 4
BACK = 8
LAYERS = 6
FORCE_CHUNK = 1024
YP = 72
W = REACH + 1
WIDE = 2 * CZ
HALF = BONDS_DEV
ENDS = 2 * BONDS_DEV

spread_cells = 1.0
mixing = 10.0
stiffness = 5.0
time_step = 0.1

F32 = jnp.float32
BF16 = jnp.bfloat16
F8 = jnp.float8_e4m3fn
NT = (((1,), (1,)), ((), ()))
NN = (((1,), (0,)), ((), ()))


def gauss_taps():
    raw_list = [
        math.exp(-0.5 * (offset - REACH) ** 2 / spread_cells**2) for offset in range(2 * REACH + 1)
    ]
    tap_total = sum(raw_list)
    return [entry / tap_total for entry in raw_list]


def mm(a, b, dims=NN):
    return lax.dot_general(a, b, dims, preferred_element_type=F32)


def two(x):
    hi = x.astype(BF16)
    return hi, (x - hi.astype(F32)).astype(BF16)


def three(x):
    hi = x.astype(BF16)
    rest = x - hi.astype(F32)
    mid = rest.astype(BF16)
    return hi, mid, (rest - mid.astype(F32)).astype(BF16)


PIECES = 3
SHRINK = 2.0**-4
WEIGHT_SCALE = 128.0


def scales(biggest):
    power = 7.0 - jnp.ceil(jnp.log2(jnp.maximum(biggest, 1e-30)))
    return jnp.exp2(power), jnp.exp2(-power)


def pieces(x, scale):
    rest = x * scale
    out = []
    for n in range(PIECES):
        out.append(rest.astype(F8))
        rest = (rest - out[-1].astype(F32)) * (1.0 / SHRINK)
    return out


def mm_pieces(table_ref, columns):
    depth = table_ref.shape[1] // PIECES
    total = mm(table_ref[:, :depth], columns[0])
    for n in range(1, PIECES):
        total = total + mm(table_ref[:, n * depth : (n + 1) * depth], columns[n])
    return total


def same8(index, rows):
    row = lax.broadcasted_iota(jnp.int32, (rows, index.shape[1]), 0)
    return row.astype(jnp.int8) == index.astype(jnp.int8)


def onehot8(index, rows):
    mask = same8(index, rows)
    return [
        jnp.where(mask, jnp.asarray(SHRINK**n, F8), jnp.zeros((), F8)) for n in range(PIECES)
    ]


def onehot8_xy(x, y):
    oys = onehot8(y, CY)
    xb = jnp.broadcast_to(x.astype(F32).astype(BF16), oys[0].shape)
    zero = jnp.zeros((), F8)
    masks = [xb == jnp.asarray(i, BF16) for i in range(CX)]
    return [jnp.concatenate([jnp.where(m, oy, zero) for m in masks], axis=0) for oy in oys]


def rows_iota(rows, n, dtype=BF16):
    return lax.broadcasted_iota(jnp.int32, (rows, n), 0).astype(F32).astype(dtype)


def onehot(index, rows):
    return jnp.where(
        rows_iota(rows, index.shape[1]) == index.astype(F32).astype(BF16),
        jnp.ones((), BF16),
        jnp.zeros((), BF16),
    )


def weighted(index, rows, value):
    return jnp.where(
        rows_iota(rows, index.shape[1]) == index.astype(F32).astype(BF16),
        value,
        jnp.zeros((), BF16),
    )


def pick(index, rows, values):
    n = index.shape[1]
    mask = lax.broadcasted_iota(jnp.int32, (rows, n), 0) == index
    return [
        jnp.sum(jnp.where(mask, values[g * rows : (g + 1) * rows], 0.0), axis=0, keepdims=True)
        for g in range(values.shape[0] // rows)
    ]


def onehot_xy(x, y, planes):
    oy = onehot(y, CY)
    xb = x.astype(F32).astype(BF16)
    zero = jnp.zeros((), BF16)
    return jnp.concatenate([jnp.where(xb == jnp.asarray(i, BF16), oy, zero) for i in planes], axis=0)


def z_operators():
    taps = gauss_taps()
    w = REACH + 1
    smooth = np.zeros((CZ + 2 * w, CZ))
    slope = np.zeros((CZ + 2 * w, CZ))
    for z in range(CZ):
        for j in range(2 * REACH + 1):
            smooth[z + w + j - REACH, z] += taps[j]
            slope[z + w + 1 + j - REACH, z] += 0.5 * taps[j]
            slope[z + w - 1 + j - REACH, z] -= 0.5 * taps[j]
    mix = np.array([[stiffness, mixing + stiffness], [mixing + stiffness, stiffness]])
    full = np.concatenate(
        [np.kron(np.eye(2), smooth), np.kron(mix.T, smooth), np.kron(mix.T, slope)], axis=1
    ).reshape(2, CZ + 2 * w, 6 * CZ)
    own = full[:, w : w + CZ].reshape(2 * CZ, 6 * CZ)
    halo = np.concatenate(
        [full[:, :w].reshape(2 * w, 6 * CZ), full[:, w + CZ :].reshape(2 * w, 6 * CZ)]
    )
    return own.astype(np.float32), halo.astype(np.float32)


def mm3(a, b_hi, b_lo):
    a_hi, a_lo = two(a)
    return mm(a_hi, b_hi) + (mm(a_hi, b_lo) + mm(a_lo, b_hi))


def to_rows(x):
    return jnp.concatenate([x[:, i : i + 128] for i in range(0, x.shape[1], 128)], axis=0)


def to_line(x):
    return jnp.concatenate([x[i : i + 1] for i in range(x.shape[0])], axis=1)


def pack(slot_ref, weight_ref, species_ref, send_ref, acc_ref):
    acc_ref[...] = jnp.zeros_like(acc_ref)

    def part(c):
        brick = slot_ref[0, pl.ds(c, 1), :]
        slot = slot_ref[1, pl.ds(c, 1), :]
        mask = same8(brick + PLANE * species_ref[...], 2 * PLANE)
        left = [
            jnp.where(mask, jnp.broadcast_to(piece, mask.shape), jnp.zeros((), F8))
            for piece in pieces(weight_ref[pl.ds(c, 1), :], WEIGHT_SCALE)
        ]
        right = jnp.where(same8(slot, SLOTS), jnp.ones((), F8), jnp.zeros((), F8))
        return mm(jnp.concatenate(left, axis=0), right, NT)

    def body(step, carry):
        acc_ref[...] += part(2 * step) + part(2 * step + 1)
        return carry

    lax.fori_loop(0, 4, body, 0)
    rows = 2 * PLANE
    total = acc_ref[(PIECES - 1) * rows :]
    for n in range(PIECES - 2, -1, -1):
        total = acc_ref[n * rows : (n + 1) * rows] + SHRINK * total
    total = total * (1.0 / WEIGHT_SCALE)
    send_ref[:, 0, :] = total[:PLANE]
    send_ref[:, 1, :] = total[PLANE:]


EDGE = tuple(range(W)) + tuple(range(CX - W, CX))
INNER = tuple(range(W, CX - W))


def spread(me, arrive, edge_done, recv_ref, cell_ref, ext_ref, xy_ref, z_ref, acc_ref):
    span = SPREAD_ROWS * SLOTS

    def source(t):
        return lax.rem(me - t + PLANE, PLANE)

    def put_z(step):
        for i in range(SPREAD_ROWS):
            t = step * SPREAD_ROWS + i
            arrive(t, source(t))
        for i in range(SPREAD_ROWS):
            p = source(step * SPREAD_ROWS + i)
            z = cell_ref[2, pl.ds(p, 1), :]
            cols = slice(i * SLOTS, (i + 1) * SLOTS)
            for k in range(2):
                hi, lo = two(recv_ref[p, k : k + 1, :])
                z_ref[step, k * CZ : (k + 1) * CZ, cols] = weighted(z, CZ, hi)
                z_ref[step, (2 + k) * CZ : (3 + k) * CZ, cols] = weighted(z, CZ, lo)

    def part(planes, with_z):
        acc_ref[...] = jnp.zeros_like(acc_ref)

        def body(step, carry):
            if with_z:
                put_z(step)
            for i in range(SPREAD_ROWS):
                p = source(step * SPREAD_ROWS + i)
                x, y = (cell_ref[a, pl.ds(p, 1), :] for a in range(2))
                xy_ref[:, i * SLOTS : (i + 1) * SLOTS] = onehot_xy(x, y, planes)
            acc_ref[...] += mm(xy_ref[...], z_ref[step], NT)
            return carry

        lax.fori_loop(0, PLANE // SPREAD_ROWS, body, 0)
        total = (acc_ref[:, :WIDE] + acc_ref[:, WIDE:]) * (CX * CY * CZ / BEADS_DEV)
        return total.reshape(len(planes), CY, WIDE)

    edge = part(EDGE, True)
    ext_ref[W : 2 * W] = edge[:W]
    ext_ref[CX : CX + W] = edge[W:]
    edge_done()
    ext_ref[2 * W : CX] = part(INNER, False)


def filter_x(ext_ref, ey_ref, head_ref, tail_ref):
    taps = gauss_taps()

    def body(i, carry):
        total = taps[0] * ext_ref[i]
        for j in range(1, 2 * REACH + 1):
            total = total + taps[j] * ext_ref[i + j]
        ey_ref[i, W : W + CY] = total
        head_ref[i] = total[:W]
        tail_ref[i] = total[CY - W :]
        return carry

    lax.fori_loop(0, CX + 2, body, 0, unroll=3)


def filter_rows(ey_ref, i, first, rows):
    taps = gauss_taps()
    total = taps[0] * ey_ref[i, first : first + rows]
    for j in range(1, 2 * REACH + 1):
        total = total + taps[j] * ey_ref[i, first + j : first + j + rows]
    return total


Y_LOW = 8
Y_HIGH = 56


def filter_y_inner(ey_ref, ay_ref):
    def body(i, carry):
        ay_ref[i, Y_LOW:Y_HIGH] = filter_rows(ey_ref, i, Y_LOW, Y_HIGH - Y_LOW)
        return carry

    lax.fori_loop(0, CX + 2, body, 0, unroll=3)


def filter_y_edge(left_ref, right_ref, ey_ref, ay_ref, head_ref, tail_ref):
    span = CY + 2
    ey_ref[:, :W] = left_ref[...]
    ey_ref[:, W + CY :] = right_ref[...]
    blank = jnp.zeros((YP - span, WIDE), F32)
    pad = jnp.zeros((WIDE - YP, WIDE), F32)

    def body(i, carry):
        low = filter_rows(ey_ref, i, 0, Y_LOW)
        high = jnp.concatenate([filter_rows(ey_ref, i, Y_HIGH, span - Y_HIGH), blank], axis=0)
        ay_ref[i, :Y_LOW] = low
        ay_ref[i, Y_HIGH:] = high
        full = jnp.concatenate([low, ay_ref[i, Y_LOW:Y_HIGH], high, pad], axis=0).T
        head_ref[i] = jnp.concatenate([full[:W], full[CZ : CZ + W]], axis=0)
        tail_ref[i] = jnp.concatenate([full[CZ - W : CZ], full[WIDE - W :]], axis=0)
        return carry

    lax.fori_loop(0, CX + 2, body, 0, unroll=3)


def filter_z_own(op_ref, ay_ref, part_ref):
    op_hi, op_lo = two(op_ref[...])
    twice = jnp.concatenate([op_hi, op_hi], axis=0)
    for i in range(0, CX + 2, LAYERS):
        hi, lo = two(ay_ref[i : i + LAYERS].reshape(LAYERS * YP, WIDE))
        own = mm(jnp.concatenate([hi, lo], axis=1), twice) + mm(hi, op_lo)
        part_ref[i : i + LAYERS] = own.reshape(LAYERS, YP, 3 * WIDE)


def slopes(
    left_ref, right_ref, hop_ref, part_ref, smooth_ref, table_ref, p_ref, pz_ref, slope_ref
):
    hop_hi, hop_lo = two(hop_ref[...])

    for i in range(0, CX + 2, LAYERS):
        halo = [
            jnp.concatenate([left_ref[q], right_ref[q]], axis=0).T[:YP]
            for q in range(i, i + LAYERS)
        ]
        both = mm3(jnp.concatenate(halo, axis=0), hop_hi, hop_lo)
        both = part_ref[i : i + LAYERS] + both.reshape(LAYERS, YP, 3 * WIDE)
        smooth_ref[i : i + LAYERS] = both[:, 1 : CY + 1, :WIDE]
        p_ref[i : i + LAYERS] = both[:, :, WIDE : 2 * WIDE]
        pz_ref[i : i + LAYERS] = both[:, :, 2 * WIDE :]
    biggest = jnp.zeros((CY, WIDE), F32)
    for q in range(1, CX + 1):
        sx = (p_ref[q + 1, 1 : CY + 1] - p_ref[q - 1, 1 : CY + 1]) * 0.5
        sy = (p_ref[q, 2 : CY + 2] - p_ref[q, :CY]) * 0.5
        sz = pz_ref[q, 1 : CY + 1]
        for a, slope in enumerate((sx, sy, sz)):
            slope_ref[a, (q - 1) * CY : q * CY] = slope
            biggest = jnp.maximum(biggest, jnp.abs(slope))
    scale, inverse = scales(jnp.max(biggest))
    for i in range(0, CX * CY, 128):
        for a in range(3):
            for n, piece in enumerate(pieces(slope_ref[a, i : i + 128].T, scale)):
                table_ref[a * WIDE : (a + 1) * WIDE, n * CX * CY + i : n * CX * CY + i + 128] = piece
    return inverse


def lookup(me, leave, table_ref, inverse, cell_ref, send_ref, a, b):
    def owners(t):
        return [lax.rem(me + 1 + t * GATHER_ROWS + i + PLANE, PLANE) for i in range(GATHER_ROWS)]

    def place(t, axis):
        return jnp.concatenate([cell_ref[axis, pl.ds(p, 1), :] for p in owners(t)], axis=1)

    def build(t, refs):
        for n, columns in enumerate(onehot8_xy(place(t, 0), place(t, 1))):
            refs[0][n] = columns

    def multiply(refs):
        refs[1][...] = mm_pieces(table_ref, refs[0][...])

    def choose(t, refs):
        found = pick(place(t, 2), CZ, refs[1][...])
        for i, p in enumerate(owners(t)):
            cols = slice(i * SLOTS, (i + 1) * SLOTS)
            blank = jnp.zeros((BACK - 6, SLOTS), F32)
            send_ref[p] = (
                jnp.concatenate([found[g][:, cols] for g in range(6)] + [blank], axis=0) * inverse
            )

    b[1][...] = jnp.zeros_like(b[1])
    build(0, a)
    steps = PLANE // GATHER_ROWS

    def body(s, carry):
        t = 2 * s
        multiply(a)
        build(t + 1, b)
        choose(t - 1, b)
        multiply(b)
        build(t + 2, a)
        choose(t, a)

        @pl.when(s > 0)
        def _():
            for p in owners(t - 1):
                leave(p)

        for p in owners(t):
            leave(p)
        return carry

    lax.fori_loop(0, steps // 2, body, 0)
    choose(steps - 1, b)
    for p in owners(steps - 1)[:-1]:
        leave(p)


def forces(recv_ref, slot_ref, weight_ref, species_ref, vel_ref, delta_ref, table_ref):
    received = recv_ref[...]
    scale, inverse = scales(jnp.max(jnp.max(jnp.abs(received), axis=0)))
    table = pltpu.einshape("dgs->gds", received)
    for g in range(6):
        for n, piece in enumerate(pieces(table[g], scale)):
            table_ref[g * PLANE : (g + 1) * PLANE, n * SLOTS : (n + 1) * SLOTS] = piece
    wide = 2 * PLANE

    def body(step, carry):
        cols = pl.ds(pl.multiple_of(step * FORCE_CHUNK, FORCE_CHUNK), FORCE_CHUNK)
        species = species_ref[:, cols]
        force = [jnp.zeros((1, FORCE_CHUNK), F32)] * 3
        for c in range(8):
            both = mm_pieces(table_ref, onehot8(slot_ref[1, c : c + 1, cols], SLOTS))
            found = pick(slot_ref[0, c : c + 1, cols] + PLANE * species, wide, both)
            weight = weight_ref[c : c + 1, cols]
            force = [force[a] - weight * found[a] for a in range(3)]
        for a in range(3):
            half = vel_ref[a : a + 1, cols] + (0.5 * time_step) * (force[a] * inverse)
            delta_ref[a : a + 1, cols] = time_step * half
        return carry

    lax.fori_loop(0, BEADS_DEV // FORCE_CHUNK, body, 0)


def bonds(pairs_ref, positions_ref, out_ref, oh_ref):
    pairs = jnp.concatenate([pairs_ref[0:1], pairs_ref[1:2]], axis=1)
    hi_index = pairs >> 7
    oh_ref[...] = onehot(pairs & 127, 128)
    number = lax.broadcasted_iota(jnp.int32, (1, HALF), 1)
    number = jnp.concatenate([number, number], axis=1)
    sign = jnp.where(lax.broadcasted_iota(jnp.int32, (1, ENDS), 1) < HALF, 1.0, -1.0)
    left = jnp.concatenate(
        [
            weighted(hi_index, 32, v.astype(F32).astype(BF16))
            for v in (number >> 6, number & 63, sign)
        ],
        axis=0,
    )
    sums = mm(left, oh_ref[...], NT).astype(BF16)
    high, low, signs = pick(hi_index, 32, mm(sums, oh_ref[...]))
    other = 64.0 * high + low - number.astype(F32)
    other_sign = signs - sign
    parts = [three(to_rows(positions_ref[a : a + 1])) for a in range(3)]
    table = [jnp.concatenate([parts[a][q] for a in range(3)], axis=0) for q in range(3)]
    oh = oh_ref[...]
    ends = pick(hi_index, 32, mm(table[0], oh) + mm(table[1], oh) + mm(table[2], oh))
    for a in range(3):
        out_ref[a : a + 1] = ends[a][:, :HALF] - ends[a][:, HALF:]
    out_ref[3:4] = other[:, :HALF]
    out_ref[4:5] = other[:, HALF:]
    out_ref[5:6] = other_sign[:, :HALF]
    out_ref[6:7] = other_sign[:, HALF:]
    out_ref[7:8] = jnp.zeros((1, HALF), F32)


def put_twice(ref, columns):
    ref[:128] = columns
    ref[128:] = columns


def constrain(pairs_ref, bonds_ref, delta_ref, pos_ref, newpos_ref, newvel_ref, oh_ref, nb_ref):
    pairs = jnp.concatenate([pairs_ref[0:1], pairs_ref[1:2]], axis=1)
    hi_index = pairs >> 7
    put_twice(oh_ref, onehot(pairs & 127, 128))
    r = [bonds_ref[a : a + 1] for a in range(3)]
    other = jnp.concatenate([bonds_ref[3:4], bonds_ref[4:5]], axis=1).astype(jnp.int32)
    sign = [bonds_ref[5:6], bonds_ref[6:7]]
    other_hi = other >> 7
    put_twice(nb_ref, onehot(other & 127, 128))
    delta = [delta_ref[a : a + 1] for a in range(3)]
    parts = [two(to_rows(d)) for d in delta]
    table = [jnp.concatenate([parts[a][q] for a in range(3)], axis=0) for q in range(2)]
    ends = pick(hi_index, 32, mm(jnp.concatenate(table, axis=1), oh_ref[...]))
    v = [r[a] + (ends[a][:, :HALF] - ends[a][:, HALF:]) for a in range(3)]
    total = [jnp.zeros((1, HALF), F32)] * 3
    for sweep in range(SWEEPS):
        vv = v[0] * v[0] + v[1] * v[1] + v[2] * v[2]
        vr = v[0] * r[0] + v[1] * r[1] + v[2] * r[2]
        g = (vv - 1.0) / (4.0 * jnp.maximum(vr, 0.5))
        shift = [g * r[a] for a in range(3)]
        total = [total[a] + shift[a] for a in range(3)]
        if sweep + 1 == SWEEPS:
            break
        pad = jnp.zeros((2, 128), F32)
        parts = [two(jnp.concatenate([to_rows(s), pad], axis=0)) for s in shift]
        table = [jnp.concatenate([parts[a][q] for a in range(3)], axis=0) for q in range(2)]
        near = pick(other_hi, 32, mm(jnp.concatenate(table, axis=1), nb_ref[...]))
        v = [
            v[a] - 2.0 * shift[a] - sign[0] * near[a][:, :HALF] + sign[1] * near[a][:, HALF:]
            for a in range(3)
        ]
    rows = []
    for a in range(3):
        both = jnp.concatenate([total[a], -total[a]], axis=1)
        rows += [weighted(hi_index, 32, q) for q in two(both)]
    moved = mm(jnp.concatenate(rows, axis=0), oh_ref[:128], NT)
    for a in range(3):
        q = to_line(moved[64 * a : 64 * a + 32] + moved[64 * a + 32 : 64 * a + 64])
        change = delta[a] - q
        newpos_ref[a : a + 1] = pos_ref[a : a + 1] + change
        newvel_ref[a : a + 1] = change / time_step


def field_kernel(
    slot_hbm,
    weight_hbm,
    species_hbm,
    cell_hbm,
    pairs_hbm,
    pos_hbm,
    op_hbm,
    hop_hbm,
    recv2_ref,
    smooth_ref,
    bonds_ref,
    acc1_ref,
    send1_ref,
    recv1_ref,
    xy_ref,
    z_ref,
    acc2_ref,
    ext_ref,
    ey_ref,
    yside_ref,
    ay_ref,
    zside_ref,
    part_ref,
    p_ref,
    pz_ref,
    s_ref,
    slope_ref,
    table_ref,
    send2_ref,
    cols_a_ref,
    found_a_ref,
    cols_b_ref,
    found_b_ref,
    oh_ref,
    slot_ref,
    weight_ref,
    species_ref,
    cell_ref,
    pairs_ref,
    pos_ref,
    op_ref,
    hop_ref,
    out_sem,
    in_sem,
    back_out_sem,
    back_in_sem,
    side_out_sem,
    side_in_sem,
    own_sem,
    input_sem,
):
    inputs = [
        pltpu.make_async_copy(src, dst, input_sem.at[n])
        for n, (src, dst) in enumerate(
            (
                (slot_hbm, slot_ref),
                (weight_hbm, weight_ref),
                (species_hbm, species_ref),
                (pairs_hbm, pairs_ref),
                (pos_hbm, pos_ref),
                (cell_hbm, cell_ref),
                (op_hbm, op_ref),
                (hop_hbm, hop_ref),
            )
        )
    ]
    for copy in inputs:
        copy.start()
    bx, by, bz = (lax.axis_index(a) for a in OWNERS)
    me = bx * N_BY + by
    counts = [lax.axis_size(a) for a in OWNERS]

    def owner(p):
        return (p // N_BY, lax.rem(p, N_BY), bz)

    def shifted(axis, by_how):
        place = [bx, by, bz]
        place[axis] = lax.rem(place[axis] + by_how + counts[axis], counts[axis])
        return tuple(place)

    barrier = pltpu.get_barrier_semaphore()

    def greet(t, carry):
        p = lax.rem(me + t, PLANE)
        pl.semaphore_signal(barrier, inc=1, device_id=owner(p), device_id_type=MESH)
        return carry

    lax.fori_loop(1, PLANE, greet, 0)
    for by_how in (-1, 1):
        pl.semaphore_signal(barrier, inc=1, device_id=shifted(2, by_how), device_id_type=MESH)

    for copy in inputs[:3]:
        copy.wait()
    pack(slot_ref, weight_ref, species_ref, send1_ref, acc1_ref)
    pl.semaphore_wait(barrier, PLANE + 1)

    def packet(send_ref, recv_ref, out, into, p, source):
        return pltpu.make_async_remote_copy(
            src_ref=send_ref.at[p],
            dst_ref=recv_ref.at[source],
            send_sem=out.at[p],
            recv_sem=into.at[source],
            device_id=owner(p),
            device_id_type=MESH,
        )

    def forward(p, source):
        return packet(send1_ref, recv1_ref, out_sem, in_sem, p, source)

    def back(p, source):
        return packet(send2_ref, recv2_ref, back_out_sem, back_in_sem, p, source)

    def send(t, carry):
        forward(lax.rem(me + t, PLANE), me).start()
        return carry

    lax.fori_loop(1, PLANE, send, 0)
    recv1_ref[me] = send1_ref[me]
    for copy in inputs[3:]:
        copy.wait()
    bonds(pairs_ref, pos_ref, bonds_ref, oh_ref)

    def arrive(t, p):
        @pl.when(t > 0)
        def _():
            forward(p, p).wait_recv()

    def sides(axis, to_left, to_right, from_left, from_right):
        return [
            pltpu.make_async_remote_copy(
                src_ref=src,
                dst_ref=dst,
                send_sem=side_out_sem.at[2 * axis + n],
                recv_sem=side_in_sem.at[2 * axis + n],
                device_id=shifted(axis, by_how),
                device_id_type=MESH,
            )
            for n, (src, dst, by_how) in enumerate(
                ((to_left, from_right, -1), (to_right, from_left, 1))
            )
        ]

    def start(copies):
        for copy in copies:
            copy.start()

    def wait(copies):
        for copy in copies:
            copy.wait()

    along_x = sides(
        0,
        ext_ref.at[pl.ds(W, W)],
        ext_ref.at[pl.ds(CX, W)],
        ext_ref.at[pl.ds(0, W)],
        ext_ref.at[pl.ds(W + CX, W)],
    )
    along_y = sides(1, *(yside_ref.at[n] for n in range(4)))
    along_z = sides(2, *(zside_ref.at[n] for n in range(4)))
    spread(
        me, arrive, lambda: start(along_x), recv1_ref, cell_ref, ext_ref, xy_ref, z_ref, acc2_ref
    )
    wait(along_x)
    filter_x(ext_ref, ey_ref, yside_ref.at[0], yside_ref.at[1])
    start(along_y)
    filter_y_inner(ey_ref, ay_ref)
    wait(along_y)
    filter_y_edge(
        yside_ref.at[2], yside_ref.at[3], ey_ref, ay_ref, zside_ref.at[0], zside_ref.at[1]
    )
    start(along_z)
    filter_z_own(op_ref, ay_ref, part_ref)
    wait(along_z)
    inverse = slopes(
        zside_ref.at[2],
        zside_ref.at[3],
        hop_ref,
        part_ref,
        s_ref,
        table_ref,
        p_ref,
        pz_ref,
        slope_ref,
    )
    keep = pltpu.make_async_copy(s_ref.at[pl.ds(1, CX)], smooth_ref, own_sem.at[0])
    keep.start()
    lookup(
        me,
        lambda p: back(p, me).start(),
        table_ref,
        inverse,
        cell_ref,
        send2_ref,
        (cols_a_ref, found_a_ref),
        (cols_b_ref, found_b_ref),
    )
    own = pltpu.make_async_copy(send2_ref.at[me], recv2_ref.at[me], own_sem.at[1])
    own.start()

    def finish(t, carry):
        p = lax.rem(me + t, PLANE)
        forward(p, me).wait_send()
        back(p, me).wait_send()
        source = lax.rem(me - t + PLANE, PLANE)
        back(source, source).wait_recv()
        return carry

    lax.fori_loop(1, PLANE, finish, 0)
    own.wait()
    keep.wait()


def bead_kernel(
    recv_ref,
    fields_ref,
    bonds_ref,
    slot_ref,
    weight_ref,
    species_ref,
    pairs_ref,
    pos_ref,
    vel_ref,
    newpos_ref,
    newvel_ref,
    smooth_ref,
    split_ref,
    table_ref,
    delta_ref,
    oh_ref,
    nb_ref,
    sem,
):
    for k in range(2):
        split_ref[k] = fields_ref[:, :, k * CZ : (k + 1) * CZ]
    keep = pltpu.make_async_copy(split_ref, smooth_ref, sem.at[0])
    keep.start()
    forces(recv_ref, slot_ref, weight_ref, species_ref, vel_ref, delta_ref, table_ref)
    constrain(pairs_ref, bonds_ref, delta_ref, pos_ref, newpos_ref, newvel_ref, oh_ref, nb_ref)
    keep.wait()


def on_device(positions, velocities, species, corner_slot, corner_weight, slot_cell, bond_pairs):
    own_op, halo_op = z_operators()
    species = species[None, :]
    layers = CX + 2
    group = GATHER_ROWS * SLOTS
    scratch = [
        ((PIECES * 2 * PLANE, SLOTS), F32),
        ((PLANE, 2, SLOTS), F32),
        ((PLANE, 2, SLOTS), F32),
        ((CX * CY // 2, SPREAD_ROWS * SLOTS), BF16),
        ((PLANE // SPREAD_ROWS, 4 * CZ, SPREAD_ROWS * SLOTS), BF16),
        ((CX * CY // 2, 4 * CZ), F32),
        ((CX + 2 * W, CY, WIDE), F32),
        ((layers, CY + 2 * W, WIDE), F32),
        ((4, layers, W, WIDE), F32),
        ((layers, YP, WIDE), F32),
        ((4, layers, 8, WIDE), F32),
        ((layers, YP, 3 * WIDE), F32),
        ((layers, YP, WIDE), F32),
        ((layers, YP, WIDE), F32),
        ((layers, CY, WIDE), F32),
        ((3, CX * CY, WIDE), F32),
        ((3 * WIDE, PIECES * CX * CY), F8),
        ((PLANE, BACK, SLOTS), F32),
        ((PIECES, CX * CY, group), F8),
        ((3 * WIDE, group), F32),
        ((PIECES, CX * CY, group), F8),
        ((3 * WIDE, group), F32),
        ((128, ENDS), BF16),
    ]
    scratch += [
        (a.shape, a.dtype)
        for a in (
            corner_slot,
            corner_weight,
            species,
            slot_cell,
            bond_pairs,
            positions,
            own_op,
            halo_op,
        )
    ]
    vmem = pl.BlockSpec(memory_space=pltpu.VMEM)
    hbm = pl.BlockSpec(memory_space=pl.ANY)
    dma = pltpu.SemaphoreType.DMA
    limit = 60 * 1024 * 1024
    returned, fields, bond_data = pl.pallas_call(
        field_kernel,
        out_shape=[
            jax.ShapeDtypeStruct((PLANE, BACK, SLOTS), F32),
            jax.ShapeDtypeStruct((CX, CY, WIDE), F32),
            jax.ShapeDtypeStruct((8, BONDS_DEV), F32),
        ],
        in_specs=[pl.BlockSpec(memory_space=pltpu.HBM)] * 8,
        out_specs=[hbm, hbm, vmem],
        scratch_shapes=[pltpu.VMEM(*s) for s in scratch]
        + [dma((PLANE,))] * 4
        + [dma((6,))] * 2
        + [dma((2,)), dma((8,))],
        compiler_params=pltpu.CompilerParams(
            vmem_limit_bytes=limit, collective_id=0, has_side_effects=True
        ),
        name="field",
    )(
        corner_slot,
        corner_weight,
        species,
        slot_cell,
        bond_pairs,
        positions,
        jnp.asarray(own_op),
        jnp.asarray(halo_op),
    )
    moved, new_velocities, smoothed = pl.pallas_call(
        bead_kernel,
        out_shape=[
            jax.ShapeDtypeStruct((3, BEADS_DEV), F32),
            jax.ShapeDtypeStruct((3, BEADS_DEV), F32),
            jax.ShapeDtypeStruct((2, CX, CY, CZ), F32),
        ],
        in_specs=[vmem] * 9,
        out_specs=[vmem, vmem, hbm],
        scratch_shapes=[
            pltpu.VMEM((2, CX, CY, CZ), F32),
            pltpu.VMEM((6 * PLANE, PIECES * SLOTS), F8),
            pltpu.VMEM((3, BEADS_DEV), F32),
            pltpu.VMEM((256, ENDS), BF16),
            pltpu.VMEM((256, ENDS), BF16),
            dma((1,)),
        ],
        compiler_params=pltpu.CompilerParams(vmem_limit_bytes=limit),
        name="bead",
    )(
        returned,
        fields,
        bond_data,
        corner_slot,
        corner_weight,
        species,
        bond_pairs,
        positions,
        velocities,
    )
    return (moved, new_velocities, smoothed)


def solution(mesh):
    placed = (
        P(None, OWNERS),
        P(None, OWNERS),
        P(OWNERS),
        P(None, None, OWNERS),
        P(None, OWNERS),
        P(None, OWNERS, None),
        P(None, OWNERS),
    )
    return jax.shard_map(
        on_device,
        mesh=mesh,
        in_specs=placed,
        out_specs=(P(None, OWNERS), P(None, OWNERS), P(None, "bx", "by", "bz")),
        check_vma=False,
    )
```
